768 devices in a mesh: sim: 32 (over z_hi, y, core), section: 24 (over x, z_lo).
Axes of the slice: x: 4, y: 8, z: 12 (z_hi: 2, z_lo: 6; z = z_hi * 6 + z_lo), core: 2. Of those that a mesh axis runs over, the one named last changes fastest.
Arguments:
- density: float32 [4, 3072, 3072], P(None, 'sim', 'section'), may hold values from 0.5 to 2
- momentum: float32 [3, 4, 3072, 3072], P(None, None, 'sim', 'section'), may hold values from -1 to 1
- energy: float32 [4, 3072, 3072], P(None, 'sim', 'section'), may hold values from 4 to 8
- membership: int32 [768, 768], P(('sim', 'section')), may hold values from 0 to 1535
- slot_of_brick: int32 [32, 24], P('sim'), may hold values from 0 to 23, each once within a row
Outputs:
- coded: float32 [5, 4, 3072, 3072], P(None, None, ('sim', 'section'))
- group_peak: float32 [5, 1536], replicated
The draws below stay inside these ranges and needn't reach their ends.
Inputs may be any that keep to these rules, and one draw needn't show every extreme that they name: `slot_of_brick`: each row is a permutation of the 24 bricks.
All inputs are finite; a program needn't handle non-finite values.
Results may differ from the reference program's by a relative error of at most 0.0003.
Values sent between devices are 32-bit elements; how exact they have to be, the bound alone decides.
A program may use at most 32 MiB of HBM per device.

```python
import jax
import jax.numpy as jnp
from jax import lax

XD = 128
ZP = 4
X = 3072
Y = 3072
GROUPS = 1536
N_SIM = 32
N_SECTION = 24


def plant(drawn, rng, low, high):
    longest = drawn.shape.index(max(drawn.shape))
    spots = []
    for shift in (0, 1):
        where = [jax.random.randint(jax.random.fold_in(rng, axis), (), 0, length) for axis, length in enumerate(drawn.shape)]
        where[longest] = (where[longest] + shift) % drawn.shape[longest]
        spots.append(tuple(where))
    return drawn.at[spots[0]].set(low).at[spots[1]].set(high)


def shard_levels(rng, dims, split, smallest, largest):
    gain = 1.0
    for dim, blocks in split:
        draws = jax.random.uniform(jax.random.fold_in(jax.random.fold_in(rng, 6), dim), (blocks,), jnp.float32, smallest / len(split), largest / len(split))
        gain = gain * jnp.repeat(jnp.exp(draws), dims[dim] // blocks).reshape((-1,) + (1,) * (len(dims) - 1 - dim))
    return gain


def setup_inputs(seed: int = 0) -> dict:
    splits = jax.random.split(jax.random.key(seed), 6)
    density = jnp.clip(0.5 + 1.5 * jax.random.uniform(splits[0], (ZP, Y, X), jnp.float32) ** shard_levels(splits[0], (ZP, Y, X), ((1, 32), (2, 24)), -0.2, 0.2), 0.5, 2.0)
    momentum = jnp.clip(jax.random.uniform(splits[1], (3, ZP, Y, X), jnp.float32, -1.0, 1.0) * shard_levels(splits[1], (3, ZP, Y, X), ((2, 32), (3, 24)), -0.4, 0.0), -1.0, 1.0)
    energy = jnp.clip(4.0 + 4.0 * jax.random.uniform(splits[2], (ZP, Y, X), jnp.float32) ** shard_levels(splits[2], (ZP, Y, X), ((1, 32), (2, 24)), -0.2, 0.2), 4.0, 8.0)
    membership = plant(jax.random.randint(splits[3], (Y // 4, X // 4), 0, GROUPS), jax.random.fold_in(splits[3], 1), 0, GROUPS - 1).astype(jnp.int32)
    slot_of_brick = jax.vmap(lambda own: jax.random.permutation(own, N_SECTION))(jax.random.split(splits[4], N_SIM)).reshape((N_SIM, N_SECTION)).astype(jnp.int32)
    return {"density": density, "momentum": momentum, "energy": energy, "membership": membership, "slot_of_brick": slot_of_brick}


GAMMA_LESS = 0.4
COURANT = 0.05
DIFFUSE = 0.1
EPSILON = 1e-06
HIGH = lax.Precision.HIGHEST

def flux_update(padded):
    density_c = padded[0]
    momentum_x = padded[1]
    momentum_y = padded[2]
    momentum_z = padded[3]
    energy_c = padded[4]
    velocity_x = momentum_x / density_c
    velocity_y = momentum_y / density_c
    kinetic = 0.5 * (momentum_x * momentum_x + momentum_y * momentum_y + momentum_z * momentum_z) / density_c
    pressure = GAMMA_LESS * (energy_c - kinetic)
    flux_x = jnp.stack([momentum_x, momentum_x * velocity_x + pressure, momentum_y * velocity_x, momentum_z * velocity_x, (energy_c + pressure) * velocity_x])
    flux_y = jnp.stack([momentum_y, momentum_x * velocity_y, momentum_y * velocity_y + pressure, momentum_z * velocity_y, (energy_c + pressure) * velocity_y])
    center = padded[:, :, 1:-1, 1:-1]
    spread = padded[:, :, 1:-1, 2:] + padded[:, :, 1:-1, :-2] + padded[:, :, 2:, 1:-1] + padded[:, :, :-2, 1:-1] - 4.0 * center
    return center - COURANT * (flux_x[:, :, 1:-1, 2:] - flux_x[:, :, 1:-1, :-2]) - COURANT * (flux_y[:, :, 2:, 1:-1] - flux_y[:, :, :-2, 1:-1]) + DIFFUSE * spread

def predict(extended):
    h = extended.shape[2] - 6
    guess = (-extended[:, :, 0:h] + 9.0 * extended[:, :, 2:h + 2] + 9.0 * extended[:, :, 4:h + 4] - extended[:, :, 6:h + 6]) / 16.0
    return extended[:, :, 3:h + 3] - guess

def cosine_entry(k, d):
    factor = jnp.where(k == 0, 0.5, jnp.sqrt(0.5))
    return factor * jnp.cos(jnp.pi * (2.0 * d + 1.0) * k / 8.0)

def cosines():
    k = jnp.arange(4, dtype=jnp.float32)[:, None]
    m = jnp.arange(4, dtype=jnp.float32)[None, :]
    return cosine_entry(k, m).astype(jnp.float32)

def brick_matrix(brick_width):
    quarter = brick_width // 4
    m = jnp.arange(brick_width, dtype=jnp.int32)[:, None]
    column = jnp.arange(brick_width, dtype=jnp.int32)[None, :]
    k = column // quarter
    j = column % quarter
    d = m - 4 * j
    entries = cosine_entry(k.astype(jnp.float32), jnp.clip(d, 0, 3).astype(jnp.float32))
    return jnp.where((d >= 0) & (d < 4), entries, 0.0).astype(jnp.float32)

def transform(residual, brick_width):
    f, z, y, x = residual.shape
    along_z = jnp.einsum('kz,fzyx->fkyx', cosines(), residual, precision=HIGH)
    blocked = along_z.reshape(f, z, y // 4, 4, x)
    along_y = jnp.einsum('km,fzbmx->fzbkx', cosines(), blocked, precision=HIGH).reshape(f, z, y, x)
    bricks = along_y.reshape(f, z, y, x // brick_width, brick_width)
    return jnp.einsum('fzybm,mc->fzybc', bricks, brick_matrix(brick_width), precision=HIGH).reshape(f, z, y, x)

def reorder(coefficients, slot_of_brick, brick_width):
    f, z, y, x = coefficients.shape
    count = x // brick_width
    slabs = slot_of_brick.shape[0]
    placing = (slot_of_brick[:, :, None] == jnp.arange(count, dtype=jnp.int32)[None, None, :]).astype(jnp.float32)
    bricks = coefficients.reshape(f, z, slabs, y // slabs, count, brick_width)
    return jnp.einsum('sbp,fzsybx->fzsypx', placing, bricks, precision=HIGH).reshape(f, z, y, x)

def block_peaks(coefficients, brick_width):
    f, z, y, x = coefficients.shape
    magnitude = lax.optimization_barrier(jnp.max(jnp.abs(coefficients), axis=1))
    magnitude = lax.optimization_barrier(jnp.max(magnitude.reshape(f, y // 4, 4, x), axis=2))
    magnitude = magnitude.reshape(f, y // 4, x // brick_width, 4, brick_width // 4)
    return lax.optimization_barrier(jnp.max(magnitude, axis=3)).reshape(f, y // 4, x // 4)

def gather_peaks(peaks, membership, groups):
    labels = jnp.arange(groups, dtype=jnp.int32)

    def visit(carry, row):
        row_peaks, row_labels = row
        matches = row_labels[:, None] == labels[None, :]
        found = lax.optimization_barrier(jnp.max(jnp.where(matches[None], row_peaks[:, :, None], 0.0), axis=1))
        return (jnp.maximum(carry, found), None)
    start = jnp.zeros((peaks.shape[0], groups), jnp.float32)
    result, unused = lax.scan(visit, start, (jnp.moveaxis(peaks, 1, 0), membership))
    return result

def spread_peaks(group_peak, membership):
    labels = jnp.arange(group_peak.shape[1], dtype=jnp.int32)

    def visit(row_labels):
        matches = (row_labels[:, None] == labels[None, :]).astype(jnp.float32)
        return jnp.dot(group_peak, matches.T, precision=HIGH)
    return jnp.moveaxis(lax.map(visit, membership), 0, 1)

def normalize(coefficients, divisor, brick_width):
    f, z, y, x = coefficients.shape
    rows_count = y // 4
    widened = divisor.reshape(f, rows_count, x // brick_width, 1, brick_width // 4)
    widened = jnp.broadcast_to(widened, (f, rows_count, x // brick_width, 4, brick_width // 4)).reshape(f, rows_count, x)
    widened = jnp.broadcast_to(widened[:, None, :, None, :], (f, z, rows_count, 4, x)).reshape(f, z, y, x)
    return coefficients / (widened + EPSILON)

def reference(density, momentum, energy, membership, slot_of_brick):
    conserved = jnp.concatenate([density[None], momentum, energy[None]], axis=0)
    padded = jnp.pad(conserved, ((0, 0), (0, 0), (1, 1), (1, 1)), mode='wrap')
    updated = flux_update(padded)
    extended = jnp.pad(updated, ((0, 0), (0, 0), (3, 3), (0, 0)), mode='wrap')
    transformed = transform(predict(extended), XD)
    placed = reorder(transformed, slot_of_brick, XD)
    peaks = block_peaks(placed, XD)
    group_peak = gather_peaks(peaks, membership, GROUPS)
    coded = normalize(placed, spread_peaks(group_peak, membership), XD)
    return (coded, group_peak)
```

```python
import functools

import jax
import jax.numpy as jnp
import numpy as np
from jax import lax
from jax.experimental import pallas as pl
from jax.experimental.pallas import tpu as pltpu
from jax.sharding import PartitionSpec as P

Z_HI, Y_CHIPS, CORES = 2, 8, 2
X_CHIPS, Z_LO = 4, 6
GAMMA_LESS, COURANT, DIFFUSE, EPSILON = 0.4, 0.05, 0.1, 1e-06
FIELDS, PLANES, LANES, EDGE = 5, 4, 128, 8
GROUPS = 1536
HIGH = lax.Precision.HIGHEST
MESH = pl.DeviceIdType.MESH


def cosines():
    k = np.arange(4)[:, None]
    m = np.arange(4)[None, :]
    return np.where(k == 0, 0.5, np.sqrt(0.5)) * np.cos(np.pi * (2 * m + 1) * k / 8)


def row_matrix(rows):
    predict = np.zeros((rows, rows + 2 * EDGE))
    for y in range(rows):
        at = y + EDGE
        predict[y, at] = 1.0
        predict[y, [at - 1, at + 1]] = -9.0 / 16.0
        predict[y, [at - 3, at + 3]] = 1.0 / 16.0
    return (np.kron(np.eye(rows // 4), cosines()) @ predict).astype(np.float32)


def brick_matrix():
    c = cosines()
    out = np.zeros((LANES, LANES))
    for j in range(LANES // 4):
        for k in range(4):
            out[4 * j : 4 * j + 4, k * (LANES // 4) + j] = c[k]
    return out.astype(np.float32)


def state_terms(c):
    rho, mx, my, mz, energy = c
    inverse = 1.0 / rho
    u = mx * inverse
    v = my * inverse
    pressure = GAMMA_LESS * (energy - 0.5 * (mx * mx + my * my + mz * mz) * inverse)
    total = energy + pressure
    flux_x = (mx, mx * u + pressure, my * u, mz * u, total * u)
    flux_y = (my, mx * v, my * v + pressure, mz * v, total * v)
    spread = [DIFFUSE * a for a in c]
    return (
        [b - COURANT * a for a, b in zip(flux_x, spread)],
        [b + COURANT * a for a, b in zip(flux_x, spread)],
        [b - COURANT * a for a, b in zip(flux_y, spread)],
        [b + COURANT * a for a, b in zip(flux_y, spread)],
    )


def step_kernel(
    slot_ref,
    density,
    momentum,
    energy,
    members,
    rows_ref,
    brick_ref,
    landed,
    final,
    ext,
    center,
    from_above,
    from_below,
    outbox,
    folded,
    member_rows,
    member_cols,
    edge_out,
    edge_in,
    edge_term,
    best,
    own,
    pass1,
    pass2,
    pass3,
    hold,
    full,
    load_sem,
    row_send,
    row_recv,
    edge_send,
    edge_recv,
    member_send,
    member_recv,
    bulk_send,
    bulk_recv,
    own_sem,
    red_send,
    red_recv,
):
    n_section = X_CHIPS * Z_LO
    n_sim = Z_HI * Y_CHIPS * CORES
    rows = 4 * n_section
    tiles = rows // 8
    s = lax.axis_index("sim")
    t = lax.axis_index("section")
    core = s % CORES
    y = (s // CORES) % Y_CHIPS
    z_hi = s // (CORES * Y_CHIPS)
    x = t // Z_LO
    z_lo = t % Z_LO
    below, above = (s + n_sim - 1) % n_sim, (s + 1) % n_sim
    left, right = (t + n_section - 1) % n_section, (t + 1) % n_section
    lane = lax.broadcasted_iota(jnp.int32, (8, LANES), 1)

    loads = [
        pltpu.make_async_copy(density, ext.at[0, :, pl.ds(EDGE, rows), :], load_sem.at[0]),
        pltpu.make_async_copy(momentum, ext.at[pl.ds(1, 3), :, pl.ds(EDGE, rows), :], load_sem.at[1]),
        pltpu.make_async_copy(energy, ext.at[4, :, pl.ds(EDGE, rows), :], load_sem.at[2]),
        pltpu.make_async_copy(members, member_rows.at[t], load_sem.at[3]),
    ]
    for copy in loads:
        copy.start()

    barrier = pltpu.get_barrier_semaphore()
    shards = CORES * X_CHIPS
    place = core * X_CHIPS + x
    z_all = Z_HI * Z_LO
    z = z_hi * Z_LO + z_lo

    def in_plane(step):
        other = (place + step) % shards
        return (s - core + other // X_CHIPS, (other % X_CHIPS) * Z_LO + z_lo)

    def in_column(step):
        return (s + ((y + step) % Y_CHIPS - y) * CORES, t)

    def in_depth(step):
        other = (z + step) % z_all
        return (s + (other // Z_LO - z_hi) * (CORES * Y_CHIPS), x * Z_LO + other % Z_LO)

    def greet(device):
        pl.semaphore_signal(barrier, inc=1, device_id=device, device_id_type=MESH)

    def greet_section(d, carry):
        greet((s, (t + d) % n_section))
        return carry

    lax.fori_loop(1, n_section, greet_section, 0)
    for sim in (below, above):
        for section in (left, t, right):
            greet((sim, section))
    for d in range(1, X_CHIPS):
        greet((s + 1 - 2 * core, ((x + d) % X_CHIPS) * Z_LO + z_lo))
    for d in range(1, Y_CHIPS):
        greet(in_column(d))
    if Z_HI > 1:
        for d in range(Z_LO):
            greet(((s + n_sim // 2) % n_sim, x * Z_LO + d))
    greetings = (n_section - 1) + 6 + (X_CHIPS - 1) + (Y_CHIPS - 1) + (Z_LO if Z_HI > 1 else 0)

    for copy in loads:
        copy.wait()

    def pack(f, carry):
        low = jnp.zeros((8, LANES), jnp.float32)
        high = jnp.zeros((8, LANES), jnp.float32)
        for plane in range(PLANES):
            for r in range(tiles):
                value = ext[f, plane, pl.ds(EDGE + 8 * r, 8), :]
                at = 4 * r + plane
                low = jnp.where(lane == at, pltpu.roll(value, at, 1) if at else value, low)
                high = jnp.where(lane == 127 - at, pltpu.roll(value, 128 - at, 1) if at else value, high)
        edge_out[0, f] = low
        edge_out[1, f] = high
        return carry

    lax.fori_loop(0, FIELDS, pack, 0)

    def cells(plane, r):
        start = pl.multiple_of(8 * r, 8) if not isinstance(r, int) else 8 * r
        c = [ext[f, plane, pl.ds(start, 8), :] for f in range(FIELDS)]
        low_x, high_x, low_y, high_y = state_terms(c)
        for f in range(FIELDS):
            up = jnp.where(lane == LANES - 1, 0.0, pltpu.roll(low_x[f], LANES - 1, 1))
            down = jnp.where(lane == 0, 0.0, pltpu.roll(high_x[f], 1, 1))
            center[f, plane, pl.ds(start, 8), :] = (1.0 - 4.0 * DIFFUSE) * c[f] + up + down
            from_above[f, plane, pl.ds(start, 8), :] = low_y[f]
            from_below[f, plane, pl.ds(start, 8), :] = high_y[f]

    def inner(plane, carry):
        def visit(r, carry):
            cells(plane, r)
            return carry

        return lax.fori_loop(1, tiles + 1, visit, carry)

    lax.fori_loop(0, PLANES, inner, 0)

    pl.semaphore_wait(barrier, greetings)

    sends = []

    def send(source, target, send_sem, recv_sem, device):
        copy = pltpu.make_async_remote_copy(
            src_ref=source, dst_ref=target, send_sem=send_sem, recv_sem=recv_sem, device_id=device, device_id_type=MESH
        )
        copy.start()
        return copy

    def arrived(ref, sem):
        pltpu.make_async_copy(ref, ref, sem).wait()

    for side, step in ((0, left), (1, right)):
        for k, sim in ((0, above), (1, s), (2, below)):
            sends.append(send(edge_out.at[side], edge_in.at[1 - side, k], edge_send.at[side, k], edge_recv.at[1 - side, k], (sim, step)))
    for i, (first, to, sim) in enumerate(((0, EDGE + rows, below), (rows - 8, 0, above))):
        sends.append(send(density.at[:, pl.ds(first, 8), :], ext.at[0, :, pl.ds(to, 8), :], row_send.at[i, 0], row_recv.at[i, 0], (sim, t)))
        sends.append(send(momentum.at[:, :, pl.ds(first, 8), :], ext.at[pl.ds(1, 3), :, pl.ds(to, 8), :], row_send.at[i, 1], row_recv.at[i, 1], (sim, t)))
        sends.append(send(energy.at[:, pl.ds(first, 8), :], ext.at[4, :, pl.ds(to, 8), :], row_send.at[i, 2], row_recv.at[i, 2], (sim, t)))

    def send_members(d, carry):
        send(members, member_rows.at[t], member_send, member_recv, (s, (t + d) % n_section))
        return carry

    lax.fori_loop(1, n_section, send_members, 0)

    for copy in sends:
        copy.wait_recv()

    def edges(k, carry):
        for side in range(2):
            c = [edge_in[side, k, f] for f in range(FIELDS)]
            terms = state_terms(c)[1 - side]
            for f in range(FIELDS):
                edge_term[side, k, f] = terms[f]
        return carry

    lax.fori_loop(0, 3, edges, 0)

    def outer(plane, carry):
        cells(plane, 0)
        cells(plane, tiles + 1)
        return carry

    lax.fori_loop(0, PLANES, outer, 0)

    c = cosines()
    a1, b1 = float(c[1, 0]), float(c[1, 1])

    def transform(f, carry):
        parts = []
        for plane in range(PLANES):
            added = []
            for r in range(tiles + 2):
                k = 0 if r == 0 else 2 if r == tiles + 1 else 1
                at = 4 * ((r - 1) % tiles) + plane
                low = pltpu.roll(edge_term[0, k, f], at + 1, 1)
                high = edge_term[1, k, f] if at == 127 else pltpu.roll(edge_term[1, k, f], 127 - at, 1)
                added.append(jnp.where(lane == 0, low, jnp.where(lane == LANES - 1, high, 0.0)))
            height = rows + 2 * EDGE
            updated = center[f, plane] + jnp.concatenate(added, axis=0)
            updated += pltpu.roll(from_above[f, plane], height - 1, 0)
            updated += pltpu.roll(from_below[f, plane], 1, 0)
            parts.append(jnp.dot(rows_ref[...], updated, precision=HIGH, preferred_element_type=jnp.float32))
        outer_sum, inner_sum = parts[0] + parts[3], parts[1] + parts[2]
        outer_gap, inner_gap = parts[0] - parts[3], parts[1] - parts[2]
        mixed = jnp.concatenate(
            [
                0.5 * (outer_sum + inner_sum),
                a1 * outer_gap + b1 * inner_gap,
                0.5 * (outer_sum - inner_sum),
                b1 * outer_gap - a1 * inner_gap,
            ],
            axis=0,
        )
        done = jnp.dot(mixed, brick_ref[...], precision=HIGH, preferred_element_type=jnp.float32)
        peak = None
        for k in range(PLANES):
            plane = done[k * rows : (k + 1) * rows]
            outbox[:, f, k] = plane.reshape(n_section, 4, LANES)
            peak = jnp.abs(plane) if peak is None else jnp.maximum(peak, jnp.abs(plane))
        peak = jnp.maximum(peak, pltpu.roll(peak, 32, 1))
        peak = jnp.maximum(peak, pltpu.roll(peak, 64, 1))
        peak = jnp.maximum(peak, pltpu.roll(peak, rows - 1, 0))
        peak = jnp.maximum(peak, pltpu.roll(peak, rows - 2, 0))
        folded[f, pl.ds(0, rows), :] = peak

        def deliver(d, carry):
            to = (t + d) % n_section
            send(outbox.at[to, f], landed.at[t, f], bulk_send, bulk_recv, (s, to))
            return carry

        lax.fori_loop(1, n_section, deliver, 0)
        pltpu.make_async_copy(outbox.at[t, f], landed.at[t, f], own_sem).start()
        return carry

    lax.fori_loop(0, FIELDS, transform, 0)

    some = pl.ds(0, n_section - 1)
    arrived(member_rows.at[some], member_recv)
    block_rows = member_cols.shape[1]
    for r in range(n_section):
        for col in range(n_section // 4):
            member_cols[col, pl.ds(r, 1), :] = member_rows[r, :, pl.ds(col * LANES, LANES)]
    slots = slot_ref[...].astype(jnp.float32)
    at = lax.broadcasted_iota(jnp.int32, slots.shape, 1)
    slot = jnp.max(jnp.where(at == t, slots, 0.0), axis=1, keepdims=True)
    slot = jnp.broadcast_to(slot, (block_rows, LANES))
    labels = jnp.full((block_rows, LANES), -1, jnp.int32)
    for p in range(n_section):
        window = member_cols[p // 4]
        turned = pltpu.roll(window, LANES - 32 * (p % 4), 1) if p % 4 else window
        labels = jnp.where(slot == float(p), turned, labels)
    peaks = [folded[f, pl.ds(0, block_rows, stride=4), :] for f in range(FIELDS)]
    best[...] = jnp.zeros(best.shape, jnp.float32)
    columns = GROUPS // LANES
    wide = lax.broadcasted_iota(jnp.int32, (block_rows, LANES), 1)

    def collect(j, carry):
        labels, peaks = carry[0], carry[1:]
        label = jnp.broadcast_to(labels[:, 0:1], (block_rows, LANES))
        spread = [jnp.broadcast_to(p[:, 0:1], (block_rows, LANES)) for p in peaks]
        for col in range(columns):
            match = label == wide + LANES * col
            for f in range(FIELDS):
                found = jnp.where(match, spread[f], 0.0)
                top = best[f, col]
                for r in range(block_rows // 8):
                    top = jnp.maximum(top, found[8 * r : 8 * r + 8])
                best[f, col] = top
        return tuple(pltpu.roll(a, LANES - 1, 1) for a in carry)

    lax.fori_loop(0, 32, collect, (labels, *peaks))

    depth = own.shape[1]
    own[...] = jnp.zeros(own.shape, jnp.float32)
    for f in range(FIELDS):
        for col in range(columns):
            at = f * columns + col
            own[at // depth, pl.ds(at % depth, 1), :] = jnp.max(best[f, col], axis=0, keepdims=True)

    for d in range(1, shards):
        other = (place + d) % shards
        send(own.at[other], pass1.at[d - 1], red_send.at[0], red_recv.at[0], in_plane(d))
    arrived(pass1, red_recv.at[0])
    value = own[place]
    for d in range(shards - 1):
        value = jnp.maximum(value, pass1[d])
    if Y_CHIPS > 1:
        hold[0] = value
        for d in range(1, Y_CHIPS):
            send(hold.at[0], pass2.at[d - 1], red_send.at[1], red_recv.at[1], in_column(d))
        arrived(pass2, red_recv.at[1])
        for d in range(Y_CHIPS - 1):
            value = jnp.maximum(value, pass2[d])
    hold[1] = value
    for d in range(1, z_all):
        send(hold.at[1], pass3.at[d - 1], red_send.at[2], red_recv.at[2], in_depth(d))
    arrived(pass3, red_recv.at[2])
    for d in range(z_all - 1):
        value = jnp.maximum(value, pass3[d])
    hold[2] = value
    for d in range(1, shards):
        send(hold.at[2], full.at[place], red_send.at[3], red_recv.at[3], in_plane(d))
    full[place] = value
    arrived(full.at[pl.ds(0, shards - 1)], red_recv.at[3])
    for i in range(shards):
        final[pl.ds(i * depth, depth), :] = full[i]

    for copy in sends:
        copy.wait_send()
    arrived(member_rows.at[some], member_send)
    arrived(outbox.at[some], bulk_send)
    arrived(pass1, red_send.at[0])
    if Y_CHIPS > 1:
        arrived(pass2, red_send.at[1])
    arrived(pass3, red_send.at[2])
    arrived(pass1, red_send.at[3])
    arrived(landed.at[0], own_sem)
    arrived(landed.at[some], bulk_recv)


def place_kernel(slot_ref, final, members, landed, coded, group_peak, peaks, scale):
    n_section = landed.shape[0]
    columns = GROUPS // LANES

    @pl.when(pl.program_id(0) == 0)
    def _():
        peaks[...] = jnp.zeros(peaks.shape, jnp.float32)
        for f in range(FIELDS):
            for col in range(columns):
                peaks[f : f + 1, col * LANES : (col + 1) * LANES] = final[f * columns + col : f * columns + col + 1, :]
        group_peak[...] = peaks[0:FIELDS, :]
        lane = lax.broadcasted_iota(jnp.int32, (8, LANES), 1)
        for block in range(n_section // 4):
            label = jnp.broadcast_to(members[0:1, block * LANES : (block + 1) * LANES], (8, LANES))
            high, low = label // LANES, label % LANES
            found = jnp.zeros((8, LANES), jnp.float32)
            for col in range(columns):
                picked = jnp.take_along_axis(
                    peaks[:, col * LANES : (col + 1) * LANES], low, axis=1, mode="promise_in_bounds"
                )
                found = jnp.where(high == col, picked, found)
            found = found + EPSILON
            turned = [found] + [pltpu.roll(found, 32 * q, 1) for q in range(1, 4)]
            for q in range(4):
                full = turned[(0 - q) % 4]
                for a in range(1, 4):
                    full = jnp.where(lane // 32 == a, turned[(a - q) % 4], full)
                for f in range(FIELDS):
                    scale[f, 4 * block + q] = full[f : f + 1]

    f = pl.program_id(0)

    for b in range(n_section):
        slot = slot_ref[0, b]
        divisor = scale[f, slot]
        coded[0, :, :, pl.ds(pl.multiple_of(slot * LANES, LANES), LANES)] = landed[b, 0] / divisor[None]


def per_device(density, momentum, energy, membership, slot_of_brick):
    planes, rows, width = density.shape
    n_section = rows // 4
    block_rows = -(-n_section // 8) * 8
    shards = CORES * X_CHIPS
    depth = 64 // shards
    f32 = jnp.float32
    height = rows + 2 * EDGE
    vmem, anywhere = pl.BlockSpec(memory_space=pltpu.VMEM), pl.BlockSpec(memory_space=pl.ANY)
    smem = pl.BlockSpec(memory_space=pltpu.SMEM)
    dma = pltpu.SemaphoreType.DMA
    landed, final = pl.pallas_call(
        step_kernel,
        out_shape=(
            jax.ShapeDtypeStruct((n_section, FIELDS, planes, 4, width), f32),
            jax.ShapeDtypeStruct((64, width), f32),
        ),
        in_specs=[vmem, anywhere, anywhere, anywhere, anywhere, vmem, vmem],
        out_specs=(anywhere, vmem),
        scratch_shapes=[
            pltpu.VMEM((FIELDS, planes, height, width), f32),
            pltpu.VMEM((FIELDS, planes, height, width), f32),
            pltpu.VMEM((FIELDS, planes, height, width), f32),
            pltpu.VMEM((FIELDS, planes, height, width), f32),
            pltpu.VMEM((n_section, FIELDS, planes, 4, width), f32),
            pltpu.VMEM((FIELDS, 4 * block_rows, width), f32),
            pltpu.VMEM((n_section, 1, membership.shape[1]), jnp.int32),
            pltpu.VMEM((n_section // 4, block_rows, width), jnp.int32),
            pltpu.VMEM((2, FIELDS, 8, width), f32),
            pltpu.VMEM((2, 3, FIELDS, 8, width), f32),
            pltpu.VMEM((2, 3, FIELDS, 8, width), f32),
            pltpu.VMEM((FIELDS, GROUPS // width, 8, width), f32),
            pltpu.VMEM((shards, depth, width), f32),
            pltpu.VMEM((shards - 1, depth, width), f32),
            pltpu.VMEM((max(Y_CHIPS - 1, 1), depth, width), f32),
            pltpu.VMEM((Z_HI * Z_LO - 1, depth, width), f32),
            pltpu.VMEM((3, depth, width), f32),
            pltpu.VMEM((shards, depth, width), f32),
            dma((4,)),
            dma((2, 3)),
            dma((2, 3)),
            dma((2, 3)),
            dma((2, 3)),
            dma,
            dma,
            dma,
            dma,
            dma,
            dma((4,)),
            dma((4,)),
        ],
        compiler_params=pltpu.CompilerParams(collective_id=0, has_side_effects=True),
        name="step",
    )(slot_of_brick, density, momentum, energy, membership, row_matrix(rows), brick_matrix())
    return pl.pallas_call(
        place_kernel,
        grid=(FIELDS,),
        out_shape=(
            jax.ShapeDtypeStruct((FIELDS, planes, 4, n_section * width), f32),
            jax.ShapeDtypeStruct((FIELDS, GROUPS), f32),
        ),
        in_specs=[
            smem,
            pl.BlockSpec((64, width), lambda f: (0, 0)),
            pl.BlockSpec(membership.shape, lambda f: (0, 0)),
            pl.BlockSpec((n_section, 1, planes, 4, width), lambda f: (0, f, 0, 0, 0)),
        ],
        out_specs=(
            pl.BlockSpec((1, planes, 4, n_section * width), lambda f: (f, 0, 0, 0)),
            pl.BlockSpec((FIELDS, GROUPS), lambda f: (0, 0)),
        ),
        scratch_shapes=[pltpu.VMEM((8, GROUPS), f32), pltpu.VMEM((FIELDS, n_section, 1, width), f32)],
        name="place",
    )(slot_of_brick, final, membership, landed)


def solution(mesh):
    placed = (
        P(None, "sim", "section"),
        P(None, None, "sim", "section"),
        P(None, "sim", "section"),
        P(("sim", "section"), None),
        P("sim", None),
    )
    return jax.shard_map(
        per_device,
        mesh=mesh,
        in_specs=placed,
        out_specs=(P(None, None, ("sim", "section"), None), P()),
        check_vma=False,
    )
```

```python
import functools

import jax
import jax.numpy as jnp
import numpy as np
from jax import lax
from jax.experimental import pallas as pl
from jax.experimental.pallas import tpu as pltpu
from jax.sharding import PartitionSpec as P

Z_HI, Y_CHIPS, CORES = 2, 8, 2
X_CHIPS, Z_LO = 4, 6
GAMMA_LESS, COURANT, DIFFUSE, EPSILON = 0.4, 0.05, 0.1, 1e-06
FIELDS, PLANES, LANES, EDGE = 5, 4, 128, 8
GROUPS = 1536
HIGH = lax.Precision.HIGHEST
MESH = pl.DeviceIdType.MESH


def cosines():
    k = np.arange(4)[:, None]
    m = np.arange(4)[None, :]
    return np.where(k == 0, 0.5, np.sqrt(0.5)) * np.cos(np.pi * (2 * m + 1) * k / 8)


def row_matrix(rows):
    predict = np.zeros((rows, rows + 2 * EDGE))
    for y in range(rows):
        at = y + EDGE
        predict[y, at] = 1.0
        predict[y, [at - 1, at + 1]] = -9.0 / 16.0
        predict[y, [at - 3, at + 3]] = 1.0 / 16.0
    return (np.kron(np.eye(rows // 4), cosines()) @ predict).astype(np.float32)


def brick_matrix():
    c = cosines()
    out = np.zeros((LANES, LANES))
    for j in range(LANES // 4):
        for k in range(4):
            out[4 * j : 4 * j + 4, k * (LANES // 4) + j] = c[k]
    return out.astype(np.float32)


def depth_matrix():
    return np.kron(np.eye(LANES // 4), cosines().T).astype(np.float32)


def state_terms(c):
    rho, mx, my, mz, energy = c
    inverse = 1.0 / rho
    u = mx * inverse
    v = my * inverse
    pressure = GAMMA_LESS * (energy - 0.5 * (mx * mx + my * my + mz * mz) * inverse)
    total = energy + pressure
    flux_x = (mx, mx * u + pressure, my * u, mz * u, total * u)
    flux_y = (my, mx * v, my * v + pressure, mz * v, total * v)
    spread = [DIFFUSE * a for a in c]
    return (
        [b - COURANT * a for a, b in zip(flux_x, spread)],
        [b + COURANT * a for a, b in zip(flux_x, spread)],
        [b - COURANT * a for a, b in zip(flux_y, spread)],
        [b + COURANT * a for a, b in zip(flux_y, spread)],
    )


def step_kernel(
    slot_ref,
    density,
    momentum,
    energy,
    members,
    rows_ref,
    brick_ref,
    depth_ref,
    landed,
    fringe,
    final,
    ext,
    center,
    from_above,
    from_below,
    outbox,
    late,
    edge_rows,
    fringe_out,
    folded,
    member_rows,
    member_cols,
    edge_out,
    edge_in,
    edge_term,
    best,
    own,
    pass1,
    pass2,
    pass3,
    hold,
    full,
    load_sem,
    row_send,
    row_recv,
    edge_send,
    edge_recv,
    member_send,
    member_recv,
    bulk_send,
    bulk_recv,
    own_sem,
    fringe_send,
    fringe_recv,
    fringe_own,
    red_send,
    red_recv,
):
    n_section = X_CHIPS * Z_LO
    n_sim = Z_HI * Y_CHIPS * CORES
    rows = 4 * n_section
    tiles = rows // 8
    s = lax.axis_index("sim")
    t = lax.axis_index("section")
    core = s % CORES
    y = (s // CORES) % Y_CHIPS
    z_hi = s // (CORES * Y_CHIPS)
    x = t // Z_LO
    z_lo = t % Z_LO
    below, above = (s + n_sim - 1) % n_sim, (s + 1) % n_sim
    left, right = (t + n_section - 1) % n_section, (t + 1) % n_section
    lane = lax.broadcasted_iota(jnp.int32, (8, LANES), 1)

    loads = [
        pltpu.make_async_copy(density, ext.at[0, :, pl.ds(EDGE, rows), :], load_sem.at[0]),
        pltpu.make_async_copy(momentum, ext.at[pl.ds(1, 3), :, pl.ds(EDGE, rows), :], load_sem.at[1]),
        pltpu.make_async_copy(energy, ext.at[4, :, pl.ds(EDGE, rows), :], load_sem.at[2]),
        pltpu.make_async_copy(members, member_rows.at[t], load_sem.at[3]),
    ]
    for copy in loads:
        copy.start()

    barrier = pltpu.get_barrier_semaphore()
    shards = CORES * X_CHIPS
    place = core * X_CHIPS + x
    z_all = Z_HI * Z_LO
    z = z_hi * Z_LO + z_lo

    def in_plane(step):
        other = (place + step) % shards
        return (s - core + other // X_CHIPS, (other % X_CHIPS) * Z_LO + z_lo)

    def in_column(step):
        return (s + ((y + step) % Y_CHIPS - y) * CORES, t)

    def in_depth(step):
        other = (z + step) % z_all
        return (s + (other // Z_LO - z_hi) * (CORES * Y_CHIPS), x * Z_LO + other % Z_LO)

    def greet(device):
        pl.semaphore_signal(barrier, inc=1, device_id=device, device_id_type=MESH)

    def greet_section(d, carry):
        greet((s, (t + d) % n_section))
        return carry

    lax.fori_loop(1, n_section, greet_section, 0)
    for sim in (below, above):
        for section in (left, t, right):
            greet((sim, section))
    for d in range(1, X_CHIPS):
        greet((s + 1 - 2 * core, ((x + d) % X_CHIPS) * Z_LO + z_lo))
    for d in range(1, Y_CHIPS):
        greet(in_column(d))
    if Z_HI > 1:
        for d in range(Z_LO):
            greet(((s + n_sim // 2) % n_sim, x * Z_LO + d))
    greetings = (n_section - 1) + 6 + (X_CHIPS - 1) + (Y_CHIPS - 1) + (Z_LO if Z_HI > 1 else 0)

    for copy in loads:
        copy.wait()

    def pack(f, carry):
        low = jnp.zeros((8, LANES), jnp.float32)
        high = jnp.zeros((8, LANES), jnp.float32)
        for plane in range(PLANES):
            for r in range(tiles):
                value = ext[f, plane, pl.ds(EDGE + 8 * r, 8), :]
                at = 4 * r + plane
                low = jnp.where(lane == at, pltpu.roll(value, at, 1) if at else value, low)
                high = jnp.where(lane == 127 - at, pltpu.roll(value, 128 - at, 1) if at else value, high)
        edge_out[0, f] = low
        edge_out[1, f] = high
        return carry

    lax.fori_loop(0, FIELDS, pack, 0)

    def cells(plane, r):
        start = pl.multiple_of(8 * r, 8) if not isinstance(r, int) else 8 * r
        c = [ext[f, plane, pl.ds(start, 8), :] for f in range(FIELDS)]
        low_x, high_x, low_y, high_y = state_terms(c)
        for f in range(FIELDS):
            up = jnp.where(lane == LANES - 1, 0.0, pltpu.roll(low_x[f], LANES - 1, 1))
            down = jnp.where(lane == 0, 0.0, pltpu.roll(high_x[f], 1, 1))
            center[f, plane, pl.ds(start, 8), :] = (1.0 - 4.0 * DIFFUSE) * c[f] + up + down
            from_above[f, plane, pl.ds(start, 8), :] = low_y[f]
            from_below[f, plane, pl.ds(start, 8), :] = high_y[f]
        return low_x, high_x

    nothing = jnp.zeros((8, LANES), jnp.float32)
    height = rows + 2 * EDGE
    for first in (0, height - 8):
        edge_rows[pl.ds(first, 8), :] = nothing
        for f in range(FIELDS):
            for plane in range(PLANES):
                for ref in (center, from_above, from_below):
                    ref[f, plane, pl.ds(first, 8), :] = nothing

    def inner(r, carry):
        packed = nothing
        for plane in range(PLANES):
            low_x, high_x = cells(plane, r)
            for f in range(FIELDS):
                at = PLANES * f + plane
                packed = jnp.where(lane == at, pltpu.roll(low_x[f], at, 1) if at else low_x[f], packed)
                packed = jnp.where(lane == 64 + at, pltpu.roll(high_x[f], 65 + at, 1), packed)
        edge_rows[pl.ds(pl.multiple_of(8 * r, 8), 8), :] = packed
        return carry

    lax.fori_loop(1, tiles + 1, inner, 0)

    def product(a, b):
        return jnp.dot(a, b, precision=HIGH, preferred_element_type=jnp.float32)

    edges_done = product(product(rows_ref[...], edge_rows[...]), depth_ref[...])
    fringe_out[...] = edges_done.reshape(n_section, 4, LANES)
    for first in (0, n_section - 1):
        fringe_out[first] = jnp.zeros((4, LANES), jnp.float32)

    def send(source, target, send_sem, recv_sem, device):
        copy = pltpu.make_async_remote_copy(
            src_ref=source, dst_ref=target, send_sem=send_sem, recv_sem=recv_sem, device_id=device, device_id_type=MESH
        )
        copy.start()

    def arrived(ref, sem):
        pltpu.make_async_copy(ref, ref, sem).wait()

    def halo_copies():
        plan = []
        for side, step in ((0, left), (1, right)):
            for k, sim in ((0, above), (1, s), (2, below)):
                plan.append((edge_out.at[side], edge_in.at[1 - side, k], edge_send.at[side, k], edge_recv.at[1 - side, k], (sim, step)))
        for i, (first, to, sim) in enumerate(((0, EDGE + rows, below), (rows - 8, 0, above))):
            plan.append((density.at[:, pl.ds(first, 8), :], ext.at[0, :, pl.ds(to, 8), :], row_send.at[i, 0], row_recv.at[i, 0], (sim, t)))
            plan.append((momentum.at[:, :, pl.ds(first, 8), :], ext.at[pl.ds(1, 3), :, pl.ds(to, 8), :], row_send.at[i, 1], row_recv.at[i, 1], (sim, t)))
            plan.append((energy.at[:, pl.ds(first, 8), :], ext.at[4, :, pl.ds(to, 8), :], row_send.at[i, 2], row_recv.at[i, 2], (sim, t)))
        return [
            pltpu.make_async_remote_copy(
                src_ref=a, dst_ref=b, send_sem=c, recv_sem=d, device_id=e, device_id_type=MESH
            )
            for a, b, c, d, e in plan
        ]

    c = cosines()
    a1, b1 = float(c[1, 0]), float(c[1, 1])

    def transformed(f, with_edges):
        parts = []
        for plane in range(PLANES):
            updated = center[f, plane]
            if with_edges:
                added = []
                for r in range(tiles + 2):
                    k = 0 if r == 0 else 2 if r == tiles + 1 else 1
                    at = 4 * ((r - 1) % tiles) + plane
                    low = pltpu.roll(edge_term[0, k, f], at + 1, 1)
                    high = edge_term[1, k, f] if at == 127 else pltpu.roll(edge_term[1, k, f], 127 - at, 1)
                    added.append(jnp.where(lane == 0, low, jnp.where(lane == LANES - 1, high, 0.0)))
                updated += jnp.concatenate(added, axis=0)
            updated += pltpu.roll(from_above[f, plane], height - 1, 0)
            updated += pltpu.roll(from_below[f, plane], 1, 0)
            parts.append(product(rows_ref[...], updated))
        outer_sum, inner_sum = parts[0] + parts[3], parts[1] + parts[2]
        outer_gap, inner_gap = parts[0] - parts[3], parts[1] - parts[2]
        mixed = jnp.concatenate(
            [
                0.5 * (outer_sum + inner_sum),
                a1 * outer_gap + b1 * inner_gap,
                0.5 * (outer_sum - inner_sum),
                b1 * outer_gap - a1 * inner_gap,
            ],
            axis=0,
        )
        done = product(mixed, brick_ref[...])
        return [done[k * rows : (k + 1) * rows] for k in range(PLANES)]

    last = n_section - 1
    is_inside = jnp.logical_and(t > 0, t < last)

    def early(f, carry):
        for k, plane in enumerate(transformed(f, False)):
            outbox[:, f, k] = plane.reshape(n_section, 4, LANES)

        @pl.when(f == 0)
        def _():
            pl.semaphore_wait(barrier, greetings)
            for copy in halo_copies():
                copy.start()

            def send_small(d, carry):
                to = (t + d) % n_section
                send(members, member_rows.at[t], member_send, member_recv, (s, to))
                send(fringe_out.at[to], fringe.at[t], fringe_send, fringe_recv, (s, to))
                return carry

            lax.fori_loop(1, n_section, send_small, 0)
            pltpu.make_async_copy(fringe_out.at[t], fringe.at[t], fringe_own).start()

        def deliver(d, carry):
            to = 1 + (t + d) % (n_section - 2)

            @pl.when(to != t)
            def _():
                send(outbox.at[to, f], landed.at[t, f], bulk_send, bulk_recv, (s, to))

            return carry

        lax.fori_loop(0, n_section - 2, deliver, 0)

        @pl.when(is_inside)
        def _():
            pltpu.make_async_copy(outbox.at[t, f], landed.at[t, f], own_sem).start()

        return carry

    lax.fori_loop(0, FIELDS, early, 0)

    for copy in halo_copies():
        copy.wait_recv()

    def edges(k, carry):
        for side in range(2):
            terms = state_terms([edge_in[side, k, f] for f in range(FIELDS)])[1 - side]
            for f in range(FIELDS):
                edge_term[side, k, f] = terms[f]
        return carry

    lax.fori_loop(0, 3, edges, 0)

    def outer(plane, carry):
        cells(plane, 0)
        cells(plane, tiles + 1)
        return carry

    lax.fori_loop(0, PLANES, outer, 0)

    def complete(f, carry):
        peak = None
        for k, plane in enumerate(transformed(f, True)):
            late[0, f, k] = plane[0:4]
            late[1, f, k] = plane[rows - 4 : rows]
            peak = jnp.abs(plane) if peak is None else jnp.maximum(peak, jnp.abs(plane))
        peak = jnp.maximum(peak, pltpu.roll(peak, 32, 1))
        peak = jnp.maximum(peak, pltpu.roll(peak, 64, 1))
        peak = jnp.maximum(peak, pltpu.roll(peak, rows - 1, 0))
        peak = jnp.maximum(peak, pltpu.roll(peak, rows - 2, 0))
        folded[f, pl.ds(0, rows), :] = peak
        for i, to in ((0, 0), (1, last)):

            @pl.when(t != to)
            def _():
                send(late.at[i, f], landed.at[t, f], bulk_send, bulk_recv, (s, to))

            @pl.when(t == to)
            def _():
                pltpu.make_async_copy(late.at[i, f], landed.at[t, f], own_sem).start()

        return carry

    lax.fori_loop(0, FIELDS, complete, 0)

    some = pl.ds(0, n_section - 1)
    arrived(member_rows.at[some], member_recv)
    block_rows = member_cols.shape[1]
    for r in range(n_section):
        for col in range(n_section // 4):
            member_cols[col, pl.ds(r, 1), :] = member_rows[r, :, pl.ds(col * LANES, LANES)]
    slots = slot_ref[...].astype(jnp.float32)
    at = lax.broadcasted_iota(jnp.int32, slots.shape, 1)
    slot = jnp.max(jnp.where(at == t, slots, 0.0), axis=1, keepdims=True)
    slot = jnp.broadcast_to(slot, (block_rows, LANES))
    labels = jnp.full((block_rows, LANES), -1, jnp.int32)
    for p in range(n_section):
        window = member_cols[p // 4]
        turned = pltpu.roll(window, LANES - 32 * (p % 4), 1) if p % 4 else window
        labels = jnp.where(slot == float(p), turned, labels)
    peaks = [folded[f, pl.ds(0, block_rows, stride=4), :] for f in range(FIELDS)]
    best[...] = jnp.zeros(best.shape, jnp.float32)
    columns = GROUPS // LANES
    wide = lax.broadcasted_iota(jnp.int32, (block_rows, LANES), 1)

    def collect(j, carry):
        labels, peaks = carry[0], carry[1:]
        label = jnp.broadcast_to(labels[:, 0:1], (block_rows, LANES))
        spread = [jnp.broadcast_to(p[:, 0:1], (block_rows, LANES)) for p in peaks]
        for col in range(columns):
            match = label == wide + LANES * col
            for f in range(FIELDS):
                found = jnp.where(match, spread[f], 0.0)
                top = best[f, col]
                for r in range(block_rows // 8):
                    top = jnp.maximum(top, found[8 * r : 8 * r + 8])
                best[f, col] = top
        return tuple(pltpu.roll(a, LANES - 1, 1) for a in carry)

    lax.fori_loop(0, 32, collect, (labels, *peaks))

    depth = own.shape[1]
    own[...] = jnp.zeros(own.shape, jnp.float32)
    for f in range(FIELDS):
        for col in range(columns):
            at = f * columns + col
            own[at // depth, pl.ds(at % depth, 1), :] = jnp.max(best[f, col], axis=0, keepdims=True)

    for d in range(1, shards):
        other = (place + d) % shards
        send(own.at[other], pass1.at[d - 1], red_send.at[0], red_recv.at[0], in_plane(d))
    arrived(pass1, red_recv.at[0])
    value = own[place]
    for d in range(shards - 1):
        value = jnp.maximum(value, pass1[d])
    if Y_CHIPS > 1:
        hold[0] = value
        for d in range(1, Y_CHIPS):
            send(hold.at[0], pass2.at[d - 1], red_send.at[1], red_recv.at[1], in_column(d))
        arrived(pass2, red_recv.at[1])
        for d in range(Y_CHIPS - 1):
            value = jnp.maximum(value, pass2[d])
    hold[1] = value
    for d in range(1, z_all):
        send(hold.at[1], pass3.at[d - 1], red_send.at[2], red_recv.at[2], in_depth(d))
    arrived(pass3, red_recv.at[2])
    for d in range(z_all - 1):
        value = jnp.maximum(value, pass3[d])
    hold[2] = value
    for d in range(1, shards):
        send(hold.at[2], full.at[place], red_send.at[3], red_recv.at[3], in_plane(d))
    full[place] = value
    arrived(full.at[pl.ds(0, shards - 1)], red_recv.at[3])
    for i in range(shards):
        final[pl.ds(i * depth, depth), :] = full[i]

    for copy in halo_copies():
        copy.wait_send()
    arrived(fringe.at[some], fringe_recv)
    arrived(fringe_out.at[some], fringe_send)
    arrived(fringe_out.at[0], fringe_own)
    arrived(member_rows.at[some], member_send)
    arrived(outbox.at[some], bulk_send)
    arrived(pass1, red_send.at[0])
    if Y_CHIPS > 1:
        arrived(pass2, red_send.at[1])
    arrived(pass3, red_send.at[2])
    arrived(pass1, red_send.at[3])
    arrived(landed.at[0], own_sem)
    arrived(landed.at[some], bulk_recv)


def place_kernel(slot_ref, final, members, landed, fringe, coded, group_peak, peaks, scale, beside, added):
    n_section = landed.shape[0]
    columns = GROUPS // LANES

    @pl.when(pl.program_id(0) == 0)
    def _():
        peaks[...] = jnp.zeros(peaks.shape, jnp.float32)
        for f in range(FIELDS):
            for col in range(columns):
                peaks[f : f + 1, col * LANES : (col + 1) * LANES] = final[f * columns + col : f * columns + col + 1, :]
        group_peak[...] = peaks[0:FIELDS, :]
        lane = lax.broadcasted_iota(jnp.int32, (8, LANES), 1)
        for block in range(n_section // 4):
            label = jnp.broadcast_to(members[0:1, block * LANES : (block + 1) * LANES], (8, LANES))
            high, low = label // LANES, label % LANES
            found = jnp.zeros((8, LANES), jnp.float32)
            for col in range(columns):
                picked = jnp.take_along_axis(
                    peaks[:, col * LANES : (col + 1) * LANES], low, axis=1, mode="promise_in_bounds"
                )
                found = jnp.where(high == col, picked, found)
            found = found + EPSILON
            turned = [found] + [pltpu.roll(found, 32 * q, 1) for q in range(1, 4)]
            for q in range(4):
                full = turned[(0 - q) % 4]
                for a in range(1, 4):
                    full = jnp.where(lane // 32 == a, turned[(a - q) % 4], full)
                for f in range(FIELDS):
                    scale[f, 4 * block + q] = full[f : f + 1]
        edges = fringe[...].reshape(4 * n_section, LANES)
        side = lax.broadcasted_iota(jnp.int32, edges.shape, 1)
        beside[...] = jnp.where(side < 64, pltpu.roll(edges, 4 * n_section - 4, 0), pltpu.roll(edges, 4, 0))

    f = pl.program_id(0)
    c = cosines()
    edges = beside[...]
    side = lax.broadcasted_iota(jnp.int32, edges.shape, 1)
    first = jnp.zeros(edges.shape, jnp.float32)
    final_cell = jnp.zeros(edges.shape, jnp.float32)
    for k in range(4):
        first = jnp.where(side == 32 * k, float(c[k, 0]), first)
        final_cell = jnp.where(side == 32 * k + 31, float(c[k, 3]), final_cell)
    for k in range(PLANES):
        extra = final_cell * edges[:, k : k + 1] + first * edges[:, 64 + k : 65 + k]
        added[:, k] = extra.reshape(n_section, 4, LANES)
    beside[...] = pltpu.roll(edges, LANES - PLANES, 1)

    for b in range(n_section):
        slot = slot_ref[0, b]
        divisor = scale[f, slot]
        coded[0, :, :, pl.ds(pl.multiple_of(slot * LANES, LANES), LANES)] = (landed[b, 0] + added[b]) / divisor[None]


def per_device(density, momentum, energy, membership, slot_of_brick):
    planes, rows, width = density.shape
    n_section = rows // 4
    block_rows = -(-n_section // 8) * 8
    shards = CORES * X_CHIPS
    depth = 64 // shards
    f32 = jnp.float32
    height = rows + 2 * EDGE
    vmem, anywhere = pl.BlockSpec(memory_space=pltpu.VMEM), pl.BlockSpec(memory_space=pl.ANY)
    smem = pl.BlockSpec(memory_space=pltpu.SMEM)
    dma = pltpu.SemaphoreType.DMA
    landed, fringe, final = pl.pallas_call(
        step_kernel,
        out_shape=(
            jax.ShapeDtypeStruct((n_section, FIELDS, planes, 4, width), f32),
            jax.ShapeDtypeStruct((n_section, 4, width), f32),
            jax.ShapeDtypeStruct((64, width), f32),
        ),
        in_specs=[vmem, anywhere, anywhere, anywhere, anywhere, vmem, vmem, vmem],
        out_specs=(anywhere, anywhere, vmem),
        scratch_shapes=[
            pltpu.VMEM((FIELDS, planes, height, width), f32),
            pltpu.VMEM((FIELDS, planes, height, width), f32),
            pltpu.VMEM((FIELDS, planes, height, width), f32),
            pltpu.VMEM((FIELDS, planes, height, width), f32),
            pltpu.VMEM((n_section, FIELDS, planes, 4, width), f32),
            pltpu.VMEM((2, FIELDS, planes, 4, width), f32),
            pltpu.VMEM((height, width), f32),
            pltpu.VMEM((n_section, 4, width), f32),
            pltpu.VMEM((FIELDS, 4 * block_rows, width), f32),
            pltpu.VMEM((n_section, 1, membership.shape[1]), jnp.int32),
            pltpu.VMEM((n_section // 4, block_rows, width), jnp.int32),
            pltpu.VMEM((2, FIELDS, 8, width), f32),
            pltpu.VMEM((2, 3, FIELDS, 8, width), f32),
            pltpu.VMEM((2, 3, FIELDS, 8, width), f32),
            pltpu.VMEM((FIELDS, GROUPS // width, 8, width), f32),
            pltpu.VMEM((shards, depth, width), f32),
            pltpu.VMEM((shards - 1, depth, width), f32),
            pltpu.VMEM((max(Y_CHIPS - 1, 1), depth, width), f32),
            pltpu.VMEM((Z_HI * Z_LO - 1, depth, width), f32),
            pltpu.VMEM((3, depth, width), f32),
            pltpu.VMEM((shards, depth, width), f32),
            dma((4,)),
            dma((2, 3)),
            dma((2, 3)),
            dma((2, 3)),
            dma((2, 3)),
            dma,
            dma,
            dma,
            dma,
            dma,
            dma,
            dma,
            dma,
            dma((4,)),
            dma((4,)),
        ],
        compiler_params=pltpu.CompilerParams(collective_id=0, has_side_effects=True),
        name="step",
    )(slot_of_brick, density, momentum, energy, membership, row_matrix(rows), brick_matrix(), depth_matrix())
    return pl.pallas_call(
        place_kernel,
        grid=(FIELDS,),
        out_shape=(
            jax.ShapeDtypeStruct((FIELDS, planes, 4, n_section * width), f32),
            jax.ShapeDtypeStruct((FIELDS, GROUPS), f32),
        ),
        in_specs=[
            smem,
            pl.BlockSpec((64, width), lambda f: (0, 0)),
            pl.BlockSpec(membership.shape, lambda f: (0, 0)),
            pl.BlockSpec((n_section, 1, planes, 4, width), lambda f: (0, f, 0, 0, 0)),
            pl.BlockSpec((n_section, 4, width), lambda f: (0, 0, 0)),
        ],
        out_specs=(
            pl.BlockSpec((1, planes, 4, n_section * width), lambda f: (f, 0, 0, 0)),
            pl.BlockSpec((FIELDS, GROUPS), lambda f: (0, 0)),
        ),
        scratch_shapes=[
            pltpu.VMEM((8, GROUPS), f32),
            pltpu.VMEM((FIELDS, n_section, 1, width), f32),
            pltpu.VMEM((rows, width), f32),
            pltpu.VMEM((n_section, planes, 4, width), f32),
        ],
        name="place",
    )(slot_of_brick, final, membership, landed, fringe)


def solution(mesh):
    placed = (
        P(None, "sim", "section"),
        P(None, None, "sim", "section"),
        P(None, "sim", "section"),
        P(("sim", "section"), None),
        P("sim", None),
    )
    return jax.shard_map(
        per_device,
        mesh=mesh,
        in_specs=placed,
        out_specs=(P(None, None, ("sim", "section"), None), P()),
        check_vma=False,
    )
```

```python
import functools

import jax
import jax.numpy as jnp
import numpy as np
from jax import lax
from jax.experimental import pallas as pl
from jax.experimental.pallas import tpu as pltpu
from jax.sharding import PartitionSpec as P

Z_HI, Y_CHIPS, CORES = 2, 8, 2
X_CHIPS, Z_LO = 4, 6
GAMMA_LESS, COURANT, DIFFUSE, EPSILON = 0.4, 0.05, 0.1, 1e-06
FIELDS, PLANES, LANES, EDGE = 5, 4, 128, 8
GROUPS = 1536
AT_ONCE = 3
HIGH = lax.Precision.HIGHEST
MESH = pl.DeviceIdType.MESH


def cosines():
    k = np.arange(4)[:, None]
    m = np.arange(4)[None, :]
    return np.where(k == 0, 0.5, np.sqrt(0.5)) * np.cos(np.pi * (2 * m + 1) * k / 8)


def row_matrix(rows):
    predict = np.zeros((rows, rows + 2 * EDGE))
    for y in range(rows):
        at = y + EDGE
        predict[y, at] = 1.0
        predict[y, [at - 1, at + 1]] = -9.0 / 16.0
        predict[y, [at - 3, at + 3]] = 1.0 / 16.0
    return (np.kron(np.eye(rows // 4), cosines()) @ predict).astype(np.float32)


def brick_matrix():
    c = cosines()
    out = np.zeros((LANES, LANES))
    for j in range(LANES // 4):
        for k in range(4):
            out[4 * j : 4 * j + 4, k * (LANES // 4) + j] = c[k]
    return out.astype(np.float32)


def depth_matrix():
    return np.kron(np.eye(LANES // 4), cosines().T).astype(np.float32)


def state_terms(c):
    rho, mx, my, mz, energy = c
    inverse = 1.0 / rho
    u = mx * inverse
    v = my * inverse
    pressure = GAMMA_LESS * (energy - 0.5 * (mx * mx + my * my + mz * mz) * inverse)
    total = energy + pressure
    flux_x = (mx, mx * u + pressure, my * u, mz * u, total * u)
    flux_y = (my, mx * v, my * v + pressure, mz * v, total * v)
    spread = [DIFFUSE * a for a in c]
    return (
        [b - COURANT * a for a, b in zip(flux_x, spread)],
        [b + COURANT * a for a, b in zip(flux_x, spread)],
        [b - COURANT * a for a, b in zip(flux_y, spread)],
        [b + COURANT * a for a, b in zip(flux_y, spread)],
    )


def step_kernel(
    slot_ref,
    density,
    momentum,
    energy,
    members,
    rows_ref,
    brick_ref,
    depth_ref,
    landed,
    fringe,
    final,
    ext,
    center,
    from_above,
    from_below,
    outbox,
    late,
    edge_rows,
    fringe_out,
    folded,
    member_rows,
    member_cols,
    edge_out,
    edge_in,
    edge_term,
    best,
    own,
    pass1,
    pass2,
    pass3,
    hold,
    full,
    load_sem,
    row_send,
    row_recv,
    edge_send,
    edge_recv,
    member_send,
    member_recv,
    bulk_send,
    bulk_recv,
    own_sem,
    fringe_send,
    fringe_recv,
    fringe_own,
    red_send,
    red_recv,
):
    n_section = X_CHIPS * Z_LO
    n_sim = Z_HI * Y_CHIPS * CORES
    rows = 4 * n_section
    tiles = rows // 8
    s = lax.axis_index("sim")
    t = lax.axis_index("section")
    core = s % CORES
    y = (s // CORES) % Y_CHIPS
    z_hi = s // (CORES * Y_CHIPS)
    x = t // Z_LO
    z_lo = t % Z_LO
    below, above = (s + n_sim - 1) % n_sim, (s + 1) % n_sim
    left, right = (t + n_section - 1) % n_section, (t + 1) % n_section
    lane = lax.broadcasted_iota(jnp.int32, (8, LANES), 1)

    loads = [
        pltpu.make_async_copy(density, ext.at[0, :, pl.ds(EDGE, rows), :], load_sem.at[0]),
        pltpu.make_async_copy(momentum, ext.at[pl.ds(1, 3), :, pl.ds(EDGE, rows), :], load_sem.at[1]),
        pltpu.make_async_copy(energy, ext.at[4, :, pl.ds(EDGE, rows), :], load_sem.at[2]),
        pltpu.make_async_copy(members, member_rows.at[t], load_sem.at[3]),
    ]
    for copy in loads:
        copy.start()

    barrier = pltpu.get_barrier_semaphore()
    shards = CORES * X_CHIPS
    place = core * X_CHIPS + x
    z_all = Z_HI * Z_LO
    z = z_hi * Z_LO + z_lo

    def in_plane(step):
        other = (place + step) % shards
        return (s - core + other // X_CHIPS, (other % X_CHIPS) * Z_LO + z_lo)

    def in_column(step):
        return (s + ((y + step) % Y_CHIPS - y) * CORES, t)

    def in_depth(step):
        other = (z + step) % z_all
        return (s + (other // Z_LO - z_hi) * (CORES * Y_CHIPS), x * Z_LO + other % Z_LO)

    def greet(device):
        pl.semaphore_signal(barrier, inc=1, device_id=device, device_id_type=MESH)

    def greet_section(d, carry):
        greet((s, (t + d) % n_section))
        return carry

    lax.fori_loop(1, n_section, greet_section, 0)
    for sim in (below, above):
        for section in (left, t, right):
            greet((sim, section))
    for d in range(1, X_CHIPS):
        greet((s + 1 - 2 * core, ((x + d) % X_CHIPS) * Z_LO + z_lo))
    for d in range(1, Y_CHIPS):
        greet(in_column(d))
    if Z_HI > 1:
        for d in range(Z_LO):
            greet(((s + n_sim // 2) % n_sim, x * Z_LO + d))
    greetings = (n_section - 1) + 6 + (X_CHIPS - 1) + (Y_CHIPS - 1) + (Z_LO if Z_HI > 1 else 0)

    for copy in loads:
        copy.wait()

    def pack(f, carry):
        low = jnp.zeros((8, LANES), jnp.float32)
        high = jnp.zeros((8, LANES), jnp.float32)
        for plane in range(PLANES):
            for r in range(tiles):
                value = ext[f, plane, pl.ds(EDGE + 8 * r, 8), :]
                at = 4 * r + plane
                low = jnp.where(lane == at, pltpu.roll(value, at, 1) if at else value, low)
                high = jnp.where(lane == 127 - at, pltpu.roll(value, 128 - at, 1) if at else value, high)
        edge_out[0, f] = low
        edge_out[1, f] = high
        return carry

    lax.fori_loop(0, FIELDS, pack, 0)

    def cells(plane, r):
        start = pl.multiple_of(8 * r, 8) if not isinstance(r, int) else 8 * r
        c = [ext[f, plane, pl.ds(start, 8), :] for f in range(FIELDS)]
        low_x, high_x, low_y, high_y = state_terms(c)
        for f in range(FIELDS):
            up = jnp.where(lane == LANES - 1, 0.0, pltpu.roll(low_x[f], LANES - 1, 1))
            down = jnp.where(lane == 0, 0.0, pltpu.roll(high_x[f], 1, 1))
            center[f, plane, pl.ds(start, 8), :] = (1.0 - 4.0 * DIFFUSE) * c[f] + up + down
            from_above[f, plane, pl.ds(start, 8), :] = low_y[f]
            from_below[f, plane, pl.ds(start, 8), :] = high_y[f]
        return low_x, high_x

    nothing = jnp.zeros((8, LANES), jnp.float32)
    height = rows + 2 * EDGE
    for first in (0, height - 8):
        edge_rows[pl.ds(first, 8), :] = nothing
        for f in range(FIELDS):
            for plane in range(PLANES):
                for ref in (center, from_above, from_below):
                    ref[f, plane, pl.ds(first, 8), :] = nothing

    def inner(r, carry):
        packed = nothing
        for plane in range(PLANES):
            low_x, high_x = cells(plane, r)
            for f in range(FIELDS):
                at = PLANES * f + plane
                packed = jnp.where(lane == at, pltpu.roll(low_x[f], at, 1) if at else low_x[f], packed)
                packed = jnp.where(lane == 64 + at, pltpu.roll(high_x[f], 65 + at, 1), packed)
        edge_rows[pl.ds(pl.multiple_of(8 * r, 8), 8), :] = packed
        return carry

    lax.fori_loop(1, tiles + 1, inner, 0)

    def product(a, b):
        return jnp.dot(a, b, precision=HIGH, preferred_element_type=jnp.float32)

    edges_done = product(product(rows_ref[...], edge_rows[...]), depth_ref[...])
    fringe_out[...] = edges_done.reshape(n_section, 4, LANES)
    for first in (0, n_section - 1):
        fringe_out[first] = jnp.zeros((4, LANES), jnp.float32)

    def send(source, target, send_sem, recv_sem, device):
        copy = pltpu.make_async_remote_copy(
            src_ref=source, dst_ref=target, send_sem=send_sem, recv_sem=recv_sem, device_id=device, device_id_type=MESH
        )
        copy.start()

    def arrived(ref, sem):
        pltpu.make_async_copy(ref, ref, sem).wait()

    def halo_copies():
        plan = []
        for side, step in ((0, left), (1, right)):
            for k, sim in ((0, above), (1, s), (2, below)):
                plan.append((edge_out.at[side], edge_in.at[1 - side, k], edge_send.at[side, k], edge_recv.at[1 - side, k], (sim, step)))
        for i, (first, to, sim) in enumerate(((0, EDGE + rows, below), (rows - 8, 0, above))):
            plan.append((density.at[:, pl.ds(first, 8), :], ext.at[0, :, pl.ds(to, 8), :], row_send.at[i, 0], row_recv.at[i, 0], (sim, t)))
            plan.append((momentum.at[:, :, pl.ds(first, 8), :], ext.at[pl.ds(1, 3), :, pl.ds(to, 8), :], row_send.at[i, 1], row_recv.at[i, 1], (sim, t)))
            plan.append((energy.at[:, pl.ds(first, 8), :], ext.at[4, :, pl.ds(to, 8), :], row_send.at[i, 2], row_recv.at[i, 2], (sim, t)))
        return [
            pltpu.make_async_remote_copy(
                src_ref=a, dst_ref=b, send_sem=c, recv_sem=d, device_id=e, device_id_type=MESH
            )
            for a, b, c, d, e in plan
        ]

    c = cosines()
    a1, b1 = float(c[1, 0]), float(c[1, 1])

    def transformed(f, with_edges):
        parts = []
        for plane in range(PLANES):
            updated = center[f, plane]
            if with_edges:
                added = []
                for r in range(tiles + 2):
                    k = 0 if r == 0 else 2 if r == tiles + 1 else 1
                    at = 4 * ((r - 1) % tiles) + plane
                    low = pltpu.roll(edge_term[0, k, f], at + 1, 1)
                    high = edge_term[1, k, f] if at == 127 else pltpu.roll(edge_term[1, k, f], 127 - at, 1)
                    added.append(jnp.where(lane == 0, low, jnp.where(lane == LANES - 1, high, 0.0)))
                updated += jnp.concatenate(added, axis=0)
            updated += pltpu.roll(from_above[f, plane], height - 1, 0)
            updated += pltpu.roll(from_below[f, plane], 1, 0)
            parts.append(product(rows_ref[...], updated))
        outer_sum, inner_sum = parts[0] + parts[3], parts[1] + parts[2]
        outer_gap, inner_gap = parts[0] - parts[3], parts[1] - parts[2]
        mixed = jnp.concatenate(
            [
                0.5 * (outer_sum + inner_sum),
                a1 * outer_gap + b1 * inner_gap,
                0.5 * (outer_sum - inner_sum),
                b1 * outer_gap - a1 * inner_gap,
            ],
            axis=0,
        )
        done = product(mixed, brick_ref[...])
        return [done[k * rows : (k + 1) * rows] for k in range(PLANES)]

    last = n_section - 1
    is_inside = jnp.logical_and(t > 0, t < last)

    def deliver(f):
        def visit(d, carry):
            to = 1 + (t + d) % (n_section - 2)

            @pl.when(to != t)
            def _():
                send(outbox.at[to, f], landed.at[t, f], bulk_send, bulk_recv, (s, to))

            return carry

        lax.fori_loop(0, n_section - 2, visit, 0)

        @pl.when(is_inside)
        def _():
            pltpu.make_async_copy(outbox.at[t, f], landed.at[t, f], own_sem).start()

    def early(f, carry):
        for k, plane in enumerate(transformed(f, False)):
            outbox[:, f, k] = plane.reshape(n_section, 4, LANES)

        @pl.when(f == 0)
        def _():
            pl.semaphore_wait(barrier, greetings)
            for copy in halo_copies():
                copy.start()

            def send_small(d, carry):
                to = (t + d) % n_section
                send(members, member_rows.at[t], member_send, member_recv, (s, to))
                send(fringe_out.at[to], fringe.at[t], fringe_send, fringe_recv, (s, to))
                return carry

            lax.fori_loop(1, n_section, send_small, 0)
            pltpu.make_async_copy(fringe_out.at[t], fringe.at[t], fringe_own).start()

        @pl.when(f < AT_ONCE)
        def _():
            deliver(f)

        return carry

    lax.fori_loop(0, FIELDS, early, 0)

    for copy in halo_copies():
        copy.wait_recv()

    def edges(k, carry):
        for side in range(2):
            terms = state_terms([edge_in[side, k, f] for f in range(FIELDS)])[1 - side]
            for f in range(FIELDS):
                edge_term[side, k, f] = terms[f]
        return carry

    lax.fori_loop(0, 3, edges, 0)

    def outer(plane, carry):
        cells(plane, 0)
        cells(plane, tiles + 1)
        return carry

    lax.fori_loop(0, PLANES, outer, 0)

    def complete(f, carry):
        peak = None
        for k, plane in enumerate(transformed(f, True)):
            late[0, f, k] = plane[0:4]
            late[1, f, k] = plane[rows - 4 : rows]
            peak = jnp.abs(plane) if peak is None else jnp.maximum(peak, jnp.abs(plane))
        peak = jnp.maximum(peak, pltpu.roll(peak, 32, 1))
        peak = jnp.maximum(peak, pltpu.roll(peak, 64, 1))
        peak = jnp.maximum(peak, pltpu.roll(peak, rows - 1, 0))
        peak = jnp.maximum(peak, pltpu.roll(peak, rows - 2, 0))
        folded[f, pl.ds(0, rows), :] = peak
        for i, to in ((0, 0), (1, last)):

            @pl.when(t != to)
            def _():
                send(late.at[i, f], landed.at[t, f], bulk_send, bulk_recv, (s, to))

            @pl.when(t == to)
            def _():
                pltpu.make_async_copy(late.at[i, f], landed.at[t, f], own_sem).start()

        return carry

    lax.fori_loop(0, FIELDS, complete, 0)

    some = pl.ds(0, n_section - 1)
    arrived(member_rows.at[some], member_recv)
    block_rows = member_cols.shape[1]
    for r in range(n_section):
        for col in range(n_section // 4):
            member_cols[col, pl.ds(r, 1), :] = member_rows[r, :, pl.ds(col * LANES, LANES)]
    slots = slot_ref[...].astype(jnp.float32)
    at = lax.broadcasted_iota(jnp.int32, slots.shape, 1)
    slot = jnp.max(jnp.where(at == t, slots, 0.0), axis=1, keepdims=True)
    slot = jnp.broadcast_to(slot, (block_rows, LANES))
    labels = jnp.full((block_rows, LANES), -1, jnp.int32)
    for p in range(n_section):
        window = member_cols[p // 4]
        turned = pltpu.roll(window, LANES - 32 * (p % 4), 1) if p % 4 else window
        labels = jnp.where(slot == float(p), turned, labels)
    peaks = [folded[f, pl.ds(0, block_rows, stride=4), :] for f in range(FIELDS)]
    best[...] = jnp.zeros(best.shape, jnp.float32)
    columns = GROUPS // LANES
    wide = lax.broadcasted_iota(jnp.int32, (block_rows, LANES), 1)

    def collect(j, carry):
        labels, peaks = carry[0], carry[1:]
        label = jnp.broadcast_to(labels[:, 0:1], (block_rows, LANES))
        spread = [jnp.broadcast_to(p[:, 0:1], (block_rows, LANES)) for p in peaks]
        for col in range(columns):
            match = label == wide + LANES * col
            for f in range(FIELDS):
                found = jnp.where(match, spread[f], 0.0)
                top = best[f, col]
                for r in range(block_rows // 8):
                    top = jnp.maximum(top, found[8 * r : 8 * r + 8])
                best[f, col] = top
        return tuple(pltpu.roll(a, LANES - 1, 1) for a in carry)

    lax.fori_loop(0, 32, collect, (labels, *peaks))

    depth = own.shape[1]
    own[...] = jnp.zeros(own.shape, jnp.float32)
    for f in range(FIELDS):
        for col in range(columns):
            at = f * columns + col
            own[at // depth, pl.ds(at % depth, 1), :] = jnp.max(best[f, col], axis=0, keepdims=True)

    for d in range(1, shards):
        other = (place + d) % shards
        send(own.at[other], pass1.at[d - 1], red_send.at[0], red_recv.at[0], in_plane(d))
    deliver(AT_ONCE)
    arrived(pass1, red_recv.at[0])
    value = own[place]
    for d in range(shards - 1):
        value = jnp.maximum(value, pass1[d])
    if Y_CHIPS > 1:
        hold[0] = value
        for d in range(1, Y_CHIPS):
            send(hold.at[0], pass2.at[d - 1], red_send.at[1], red_recv.at[1], in_column(d))
        arrived(pass2, red_recv.at[1])
        for d in range(Y_CHIPS - 1):
            value = jnp.maximum(value, pass2[d])
    hold[1] = value
    for d in range(1, z_all):
        send(hold.at[1], pass3.at[d - 1], red_send.at[2], red_recv.at[2], in_depth(d))
    for f in range(AT_ONCE + 1, FIELDS):
        deliver(f)
    arrived(pass3, red_recv.at[2])
    for d in range(z_all - 1):
        value = jnp.maximum(value, pass3[d])
    hold[2] = value
    for d in range(1, shards):
        send(hold.at[2], full.at[place], red_send.at[3], red_recv.at[3], in_plane(d))
    full[place] = value
    arrived(full.at[pl.ds(0, shards - 1)], red_recv.at[3])
    for i in range(shards):
        final[pl.ds(i * depth, depth), :] = full[i]

    for copy in halo_copies():
        copy.wait_send()
    arrived(fringe.at[some], fringe_recv)
    arrived(fringe_out.at[some], fringe_send)
    arrived(fringe_out.at[0], fringe_own)
    arrived(member_rows.at[some], member_send)
    arrived(outbox.at[some], bulk_send)
    arrived(pass1, red_send.at[0])
    if Y_CHIPS > 1:
        arrived(pass2, red_send.at[1])
    arrived(pass3, red_send.at[2])
    arrived(pass1, red_send.at[3])
    arrived(landed.at[0], own_sem)
    arrived(landed.at[some], bulk_recv)


def place_kernel(slot_ref, final, members, landed, fringe, coded, group_peak, peaks, scale, beside, added):
    n_section = landed.shape[0]
    columns = GROUPS // LANES

    @pl.when(pl.program_id(0) == 0)
    def _():
        peaks[...] = jnp.zeros(peaks.shape, jnp.float32)
        for f in range(FIELDS):
            for col in range(columns):
                peaks[f : f + 1, col * LANES : (col + 1) * LANES] = final[f * columns + col : f * columns + col + 1, :]
        group_peak[...] = peaks[0:FIELDS, :]
        lane = lax.broadcasted_iota(jnp.int32, (8, LANES), 1)
        for block in range(n_section // 4):
            label = jnp.broadcast_to(members[0:1, block * LANES : (block + 1) * LANES], (8, LANES))
            high, low = label // LANES, label % LANES
            found = jnp.zeros((8, LANES), jnp.float32)
            for col in range(columns):
                picked = jnp.take_along_axis(
                    peaks[:, col * LANES : (col + 1) * LANES], low, axis=1, mode="promise_in_bounds"
                )
                found = jnp.where(high == col, picked, found)
            found = 1.0 / (found + EPSILON)
            turned = [found] + [pltpu.roll(found, 32 * q, 1) for q in range(1, 4)]
            for q in range(4):
                full = turned[(0 - q) % 4]
                for a in range(1, 4):
                    full = jnp.where(lane // 32 == a, turned[(a - q) % 4], full)
                for f in range(FIELDS):
                    scale[f, 4 * block + q] = full[f : f + 1]
        edges = fringe[...].reshape(4 * n_section, LANES)
        side = lax.broadcasted_iota(jnp.int32, edges.shape, 1)
        beside[...] = jnp.where(side < 64, pltpu.roll(edges, 4 * n_section - 4, 0), pltpu.roll(edges, 4, 0))

    f = pl.program_id(0)
    c = cosines()
    edges = beside[...]
    side = lax.broadcasted_iota(jnp.int32, edges.shape, 1)
    first = jnp.zeros(edges.shape, jnp.float32)
    final_cell = jnp.zeros(edges.shape, jnp.float32)
    for k in range(4):
        first = jnp.where(side == 32 * k, float(c[k, 0]), first)
        final_cell = jnp.where(side == 32 * k + 31, float(c[k, 3]), final_cell)
    for k in range(PLANES):
        extra = final_cell * edges[:, k : k + 1] + first * edges[:, 64 + k : 65 + k]
        added[:, k] = extra.reshape(n_section, 4, LANES)
    beside[...] = pltpu.roll(edges, LANES - PLANES, 1)

    for b in range(n_section):
        slot = slot_ref[0, b]
        factor = scale[f, slot]
        coded[0, :, :, pl.ds(pl.multiple_of(slot * LANES, LANES), LANES)] = (landed[b, 0] + added[b]) * factor[None]


def per_device(density, momentum, energy, membership, slot_of_brick):
    planes, rows, width = density.shape
    n_section = rows // 4
    block_rows = -(-n_section // 8) * 8
    shards = CORES * X_CHIPS
    depth = 64 // shards
    f32 = jnp.float32
    height = rows + 2 * EDGE
    vmem, anywhere = pl.BlockSpec(memory_space=pltpu.VMEM), pl.BlockSpec(memory_space=pl.ANY)
    smem = pl.BlockSpec(memory_space=pltpu.SMEM)
    dma = pltpu.SemaphoreType.DMA
    landed, fringe, final = pl.pallas_call(
        step_kernel,
        out_shape=(
            jax.ShapeDtypeStruct((n_section, FIELDS, planes, 4, width), f32),
            jax.ShapeDtypeStruct((n_section, 4, width), f32),
            jax.ShapeDtypeStruct((64, width), f32),
        ),
        in_specs=[vmem, anywhere, anywhere, anywhere, anywhere, vmem, vmem, vmem],
        out_specs=(anywhere, anywhere, vmem),
        scratch_shapes=[
            pltpu.VMEM((FIELDS, planes, height, width), f32),
            pltpu.VMEM((FIELDS, planes, height, width), f32),
            pltpu.VMEM((FIELDS, planes, height, width), f32),
            pltpu.VMEM((FIELDS, planes, height, width), f32),
            pltpu.VMEM((n_section, FIELDS, planes, 4, width), f32),
            pltpu.VMEM((2, FIELDS, planes, 4, width), f32),
            pltpu.VMEM((height, width), f32),
            pltpu.VMEM((n_section, 4, width), f32),
            pltpu.VMEM((FIELDS, 4 * block_rows, width), f32),
            pltpu.VMEM((n_section, 1, membership.shape[1]), jnp.int32),
            pltpu.VMEM((n_section // 4, block_rows, width), jnp.int32),
            pltpu.VMEM((2, FIELDS, 8, width), f32),
            pltpu.VMEM((2, 3, FIELDS, 8, width), f32),
            pltpu.VMEM((2, 3, FIELDS, 8, width), f32),
            pltpu.VMEM((FIELDS, GROUPS // width, 8, width), f32),
            pltpu.VMEM((shards, depth, width), f32),
            pltpu.VMEM((shards - 1, depth, width), f32),
            pltpu.VMEM((max(Y_CHIPS - 1, 1), depth, width), f32),
            pltpu.VMEM((Z_HI * Z_LO - 1, depth, width), f32),
            pltpu.VMEM((3, depth, width), f32),
            pltpu.VMEM((shards, depth, width), f32),
            dma((4,)),
            dma((2, 3)),
            dma((2, 3)),
            dma((2, 3)),
            dma((2, 3)),
            dma,
            dma,
            dma,
            dma,
            dma,
            dma,
            dma,
            dma,
            dma((4,)),
            dma((4,)),
        ],
        compiler_params=pltpu.CompilerParams(collective_id=0, has_side_effects=True),
        name="step",
    )(slot_of_brick, density, momentum, energy, membership, row_matrix(rows), brick_matrix(), depth_matrix())
    return pl.pallas_call(
        place_kernel,
        grid=(FIELDS,),
        out_shape=(
            jax.ShapeDtypeStruct((FIELDS, planes, 4, n_section * width), f32),
            jax.ShapeDtypeStruct((FIELDS, GROUPS), f32),
        ),
        in_specs=[
            smem,
            pl.BlockSpec((64, width), lambda f: (0, 0)),
            pl.BlockSpec(membership.shape, lambda f: (0, 0)),
            pl.BlockSpec((n_section, 1, planes, 4, width), lambda f: (0, f, 0, 0, 0)),
            pl.BlockSpec((n_section, 4, width), lambda f: (0, 0, 0)),
        ],
        out_specs=(
            pl.BlockSpec((1, planes, 4, n_section * width), lambda f: (f, 0, 0, 0)),
            pl.BlockSpec((FIELDS, GROUPS), lambda f: (0, 0)),
        ),
        scratch_shapes=[
            pltpu.VMEM((8, GROUPS), f32),
            pltpu.VMEM((FIELDS, n_section, 1, width), f32),
            pltpu.VMEM((rows, width), f32),
            pltpu.VMEM((n_section, planes, 4, width), f32),
        ],
        name="place",
    )(slot_of_brick, final, membership, landed, fringe)


def solution(mesh):
    placed = (
        P(None, "sim", "section"),
        P(None, None, "sim", "section"),
        P(None, "sim", "section"),
        P(("sim", "section"), None),
        P("sim", None),
    )
    return jax.shard_map(
        per_device,
        mesh=mesh,
        in_specs=placed,
        out_specs=(P(None, None, ("sim", "section"), None), P()),
        check_vma=False,
    )
```

```python
import functools

import jax
import jax.numpy as jnp
import numpy as np
from jax import lax
from jax.experimental import pallas as pl
from jax.experimental.pallas import tpu as pltpu
from jax.sharding import PartitionSpec as P

Z_HI, Y_CHIPS, CORES = 2, 8, 2
X_CHIPS, Z_LO = 4, 6
GAMMA_LESS, COURANT, DIFFUSE, EPSILON = 0.4, 0.05, 0.1, 1e-06
FIELDS, PLANES, LANES, EDGE = 5, 4, 128, 8
GROUPS = 1536
HIGH = lax.Precision.HIGHEST
MESH = pl.DeviceIdType.MESH


def cosines():
    k = np.arange(4)[:, None]
    m = np.arange(4)[None, :]
    return np.where(k == 0, 0.5, np.sqrt(0.5)) * np.cos(np.pi * (2 * m + 1) * k / 8)


def row_matrix(rows):
    predict = np.zeros((rows, rows + 2 * EDGE))
    for y in range(rows):
        at = y + EDGE
        predict[y, at] = 1.0
        predict[y, [at - 1, at + 1]] = -9.0 / 16.0
        predict[y, [at - 3, at + 3]] = 1.0 / 16.0
    return (np.kron(np.eye(rows // 4), cosines()) @ predict).astype(np.float32)


def outer_matrix(rows):
    whole = row_matrix(rows)
    out = np.zeros((8, 32), np.float32)
    out[:4, :16] = whole[:4, :16]
    out[4:, 16:] = whole[rows - 4 :, rows:]
    return out


def brick_matrix():
    c = cosines()
    out = np.zeros((LANES, LANES))
    for j in range(LANES // 4):
        for k in range(4):
            out[4 * j : 4 * j + 4, k * (LANES // 4) + j] = c[k]
    return out.astype(np.float32)


def depth_matrix():
    return np.kron(np.eye(LANES // 4), cosines().T).astype(np.float32)


def state_terms(c):
    rho, mx, my, mz, energy = c
    inverse = 1.0 / rho
    u = mx * inverse
    v = my * inverse
    pressure = GAMMA_LESS * (energy - 0.5 * (mx * mx + my * my + mz * mz) * inverse)
    total = energy + pressure
    flux_x = (mx, mx * u + pressure, my * u, mz * u, total * u)
    flux_y = (my, mx * v, my * v + pressure, mz * v, total * v)
    spread = [DIFFUSE * a for a in c]
    return (
        [b - COURANT * a for a, b in zip(flux_x, spread)],
        [b + COURANT * a for a, b in zip(flux_x, spread)],
        [b - COURANT * a for a, b in zip(flux_y, spread)],
        [b + COURANT * a for a, b in zip(flux_y, spread)],
    )


def step_kernel(
    slot_ref,
    density,
    momentum,
    energy,
    members,
    rows_ref,
    brick_ref,
    depth_ref,
    outer_ref,
    landed,
    fringe,
    final,
    ext,
    center,
    from_above,
    from_below,
    outbox,
    late,
    edge_rows,
    planes_done,
    beside,
    beyond_mixed,
    fringe_out,
    folded,
    member_rows,
    member_cols,
    edge_out,
    edge_in,
    edge_term,
    best,
    own,
    pass1,
    pass2,
    pass3,
    hold,
    full,
    load_sem,
    row_send,
    row_recv,
    edge_send,
    edge_recv,
    member_send,
    member_recv,
    bulk_send,
    bulk_recv,
    own_sem,
    fringe_send,
    fringe_recv,
    fringe_own,
    red_send,
    red_recv,
):
    n_section = X_CHIPS * Z_LO
    n_sim = Z_HI * Y_CHIPS * CORES
    rows = 4 * n_section
    tiles = rows // 8
    s = lax.axis_index("sim")
    t = lax.axis_index("section")
    core = s % CORES
    y = (s // CORES) % Y_CHIPS
    z_hi = s // (CORES * Y_CHIPS)
    x = t // Z_LO
    z_lo = t % Z_LO
    below, above = (s + n_sim - 1) % n_sim, (s + 1) % n_sim
    left, right = (t + n_section - 1) % n_section, (t + 1) % n_section
    lane = lax.broadcasted_iota(jnp.int32, (8, LANES), 1)

    loads = [
        pltpu.make_async_copy(density, ext.at[0, :, pl.ds(EDGE, rows), :], load_sem.at[0]),
        pltpu.make_async_copy(momentum, ext.at[pl.ds(1, 3), :, pl.ds(EDGE, rows), :], load_sem.at[1]),
        pltpu.make_async_copy(energy, ext.at[4, :, pl.ds(EDGE, rows), :], load_sem.at[2]),
        pltpu.make_async_copy(members, member_rows.at[t], load_sem.at[3]),
    ]
    for copy in loads:
        copy.start()

    barrier = pltpu.get_barrier_semaphore()
    shards = CORES * X_CHIPS
    place = core * X_CHIPS + x
    z_all = Z_HI * Z_LO
    z = z_hi * Z_LO + z_lo

    def in_plane(step):
        other = (place + step) % shards
        return (s - core + other // X_CHIPS, (other % X_CHIPS) * Z_LO + z_lo)

    def in_column(step):
        return (s + ((y + step) % Y_CHIPS - y) * CORES, t)

    def in_depth(step):
        other = (z + step) % z_all
        return (s + (other // Z_LO - z_hi) * (CORES * Y_CHIPS), x * Z_LO + other % Z_LO)

    def greet(device):
        pl.semaphore_signal(barrier, inc=1, device_id=device, device_id_type=MESH)

    def greet_section(d, carry):
        greet((s, (t + d) % n_section))
        return carry

    lax.fori_loop(1, n_section, greet_section, 0)
    for sim in (below, above):
        for section in (left, t, right):
            greet((sim, section))
    for d in range(1, X_CHIPS):
        greet((s + 1 - 2 * core, ((x + d) % X_CHIPS) * Z_LO + z_lo))
    for d in range(1, Y_CHIPS):
        greet(in_column(d))
    if Z_HI > 1:
        for d in range(Z_LO):
            greet(((s + n_sim // 2) % n_sim, x * Z_LO + d))
    greetings = (n_section - 1) + 6 + (X_CHIPS - 1) + (Y_CHIPS - 1) + (Z_LO if Z_HI > 1 else 0)

    for copy in loads:
        copy.wait()

    def pack(f, carry):
        low = jnp.zeros((8, LANES), jnp.float32)
        high = jnp.zeros((8, LANES), jnp.float32)
        for plane in range(PLANES):
            for r in range(tiles):
                value = ext[f, plane, pl.ds(EDGE + 8 * r, 8), :]
                at = 4 * r + plane
                low = jnp.where(lane == at, pltpu.roll(value, at, 1) if at else value, low)
                high = jnp.where(lane == at, pltpu.roll(value, at + 1, 1), high)
        edge_out[0, f] = low
        edge_out[1, f] = high
        return carry

    lax.fori_loop(0, FIELDS, pack, 0)

    def cells(plane, r):
        start = pl.multiple_of(8 * r, 8) if not isinstance(r, int) else 8 * r
        c = [ext[f, plane, pl.ds(start, 8), :] for f in range(FIELDS)]
        low_x, high_x, low_y, high_y = state_terms(c)
        for f in range(FIELDS):
            up = jnp.where(lane == LANES - 1, 0.0, pltpu.roll(low_x[f], LANES - 1, 1))
            down = jnp.where(lane == 0, 0.0, pltpu.roll(high_x[f], 1, 1))
            center[f, plane, pl.ds(start, 8), :] = (1.0 - 4.0 * DIFFUSE) * c[f] + up + down
            from_above[f, plane, pl.ds(start, 8), :] = low_y[f]
            from_below[f, plane, pl.ds(start, 8), :] = high_y[f]
        return low_x, high_x

    nothing = jnp.zeros((8, LANES), jnp.float32)
    height = rows + 2 * EDGE
    for first in (0, height - 8):
        edge_rows[pl.ds(first, 8), :] = nothing
        for f in range(FIELDS):
            for plane in range(PLANES):
                for ref in (center, from_above, from_below):
                    ref[f, plane, pl.ds(first, 8), :] = nothing

    def inner(r, carry):
        packed = nothing
        for plane in range(PLANES):
            low_x, high_x = cells(plane, r)
            for f in range(FIELDS):
                at = PLANES * f + plane
                packed = jnp.where(lane == at, pltpu.roll(low_x[f], at, 1) if at else low_x[f], packed)
                packed = jnp.where(lane == 64 + at, pltpu.roll(high_x[f], 65 + at, 1), packed)
        edge_rows[pl.ds(pl.multiple_of(8 * r, 8), 8), :] = packed
        return carry

    lax.fori_loop(1, tiles + 1, inner, 0)

    def product(a, b):
        return jnp.dot(a, b, precision=HIGH, preferred_element_type=jnp.float32)

    edges_done = product(product(rows_ref[...], edge_rows[...]), depth_ref[...])
    fringe_out[...] = edges_done.reshape(n_section, 4, LANES)
    for first in (0, n_section - 1):
        fringe_out[first] = jnp.zeros((4, LANES), jnp.float32)

    def send(source, target, send_sem, recv_sem, device):
        copy = pltpu.make_async_remote_copy(
            src_ref=source, dst_ref=target, send_sem=send_sem, recv_sem=recv_sem, device_id=device, device_id_type=MESH
        )
        copy.start()

    def arrived(ref, sem):
        pltpu.make_async_copy(ref, ref, sem).wait()

    def halo_copies():
        plan = []
        for side, step in ((0, left), (1, right)):
            for k, sim in ((0, above), (1, s), (2, below)):
                plan.append((edge_out.at[side], edge_in.at[1 - side, k], edge_send.at[side, k], edge_recv.at[1 - side, k], (sim, step)))
        for i, (first, to, sim) in enumerate(((0, EDGE + rows, below), (rows - 8, 0, above))):
            plan.append((density.at[:, pl.ds(first, 8), :], ext.at[0, :, pl.ds(to, 8), :], row_send.at[i, 0], row_recv.at[i, 0], (sim, t)))
            plan.append((momentum.at[:, :, pl.ds(first, 8), :], ext.at[pl.ds(1, 3), :, pl.ds(to, 8), :], row_send.at[i, 1], row_recv.at[i, 1], (sim, t)))
            plan.append((energy.at[:, pl.ds(first, 8), :], ext.at[4, :, pl.ds(to, 8), :], row_send.at[i, 2], row_recv.at[i, 2], (sim, t)))
        return [
            pltpu.make_async_remote_copy(
                src_ref=a, dst_ref=b, send_sem=c, recv_sem=d, device_id=e, device_id_type=MESH
            )
            for a, b, c, d, e in plan
        ]

    c = cosines()
    a1, b1 = float(c[1, 0]), float(c[1, 1])

    def mix(parts):
        outer_sum, inner_sum = parts[0] + parts[3], parts[1] + parts[2]
        outer_gap, inner_gap = parts[0] - parts[3], parts[1] - parts[2]
        return jnp.concatenate(
            [
                0.5 * (outer_sum + inner_sum),
                a1 * outer_gap + b1 * inner_gap,
                0.5 * (outer_sum - inner_sum),
                b1 * outer_gap - a1 * inner_gap,
            ],
            axis=0,
        )

    def transformed(f):
        parts = []
        for plane in range(PLANES):
            updated = center[f, plane] + pltpu.roll(from_above[f, plane], height - 1, 0)
            updated += pltpu.roll(from_below[f, plane], 1, 0)
            parts.append(product(rows_ref[...], updated))
        done = product(mix(parts), brick_ref[...])
        return [done[k * rows : (k + 1) * rows] for k in range(PLANES)]

    last = n_section - 1
    is_inside = jnp.logical_and(t > 0, t < last)

    def deliver(first, count):
        some_fields = pl.ds(first, count)

        def visit(d, carry):
            to = 1 + (t + d) % (n_section - 2)

            @pl.when(to != t)
            def _():
                send(outbox.at[to, some_fields], landed.at[t, some_fields], bulk_send, bulk_recv, (s, to))

            return carry

        lax.fori_loop(0, n_section - 2, visit, 0)

        @pl.when(is_inside)
        def _():
            pltpu.make_async_copy(outbox.at[t, some_fields], landed.at[t, some_fields], own_sem).start()

    def early(f, carry):
        for k, plane in enumerate(transformed(f)):
            outbox[:, f, k] = plane.reshape(n_section, 4, LANES)
            planes_done[f, k] = plane

        @pl.when(f == 0)
        def _():
            pl.semaphore_wait(barrier, greetings)
            for copy in halo_copies():
                copy.start()

            def send_small(d, carry):
                to = (t + d) % n_section
                send(members, member_rows.at[t], member_send, member_recv, (s, to))
                send(fringe_out.at[to], fringe.at[t], fringe_send, fringe_recv, (s, to))
                return carry

            lax.fori_loop(1, n_section, send_small, 0)
            pltpu.make_async_copy(fringe_out.at[t], fringe.at[t], fringe_own).start()

        @pl.when(f == 2)
        def _():
            deliver(0, 3)

        return carry

    lax.fori_loop(0, FIELDS, early, 0)

    for copy in halo_copies():
        copy.wait_recv()

    def edges(k, carry):
        for side in range(2):
            terms = state_terms([edge_in[side, k, f] for f in range(FIELDS)])[1 - side]
            for f in range(FIELDS):
                edge_term[side, k, f] = terms[f]
        return carry

    lax.fori_loop(0, 3, edges, 0)

    def outer(plane, carry):
        cells(plane, 0)
        cells(plane, tiles + 1)
        return carry

    lax.fori_loop(0, PLANES, outer, 0)

    group = lane // PLANES
    for r in range(tiles + 2):
        k = 0 if r == 0 else 2 if r == tiles + 1 else 1
        at = (r - 1) % tiles
        packed = nothing
        for f in range(FIELDS):
            packed = jnp.where(group == f, pltpu.roll(edge_term[1, k, f], (4 * (f - at)) % LANES, 1), packed)
            packed = jnp.where(group == 16 + f, pltpu.roll(edge_term[0, k, f], (64 + 4 * (f - at)) % LANES, 1), packed)
        edge_rows[pl.ds(8 * r, 8), :] = packed
    beside[...] = product(product(rows_ref[...], edge_rows[...]), depth_ref[...])

    def beyond(f, carry):
        parts = []
        for plane in range(PLANES):
            halves = []
            for first, low in ((0, True), (height - 8, False)):
                tile = [ref[f, plane, pl.ds(first, 8), :] for ref in (center, from_above, from_below)]
                both = [jnp.concatenate([a, nothing] if low else [nothing, a], axis=0) for a in tile]
                halves.append(both[0] + pltpu.roll(both[1], 15, 0) + pltpu.roll(both[2], 1, 0))
            parts.append(jnp.concatenate(halves, axis=0))
        made = product(outer_ref[...], jnp.concatenate(parts, axis=1))
        beyond_mixed[pl.ds(pl.multiple_of(32 * f, 32), 32), :] = mix(
            [made[:, LANES * k : LANES * (k + 1)] for k in range(PLANES)]
        )
        return carry

    lax.fori_loop(0, FIELDS, beyond, 0)
    beyond_mixed[...] = product(beyond_mixed[...], brick_ref[...])

    wide_lane = lax.broadcasted_iota(jnp.int32, (rows, LANES), 1)
    first_cell = jnp.zeros((rows, LANES), jnp.float32)
    final_cell = jnp.zeros((rows, LANES), jnp.float32)
    for k in range(4):
        first_cell = jnp.where(wide_lane == 32 * k, float(c[k, 0]), first_cell)
        final_cell = jnp.where(wide_lane == 32 * k + 31, float(c[k, 3]), final_cell)
    upper = lax.broadcasted_iota(jnp.int32, (8, LANES), 0) < 4

    def complete(f, carry):
        peak = None
        columns_now = beside[...]
        for k in range(PLANES):
            plane = planes_done[f, k] + final_cell * columns_now[:, k : k + 1] + first_cell * columns_now[:, 64 + k : 65 + k]
            outside = beyond_mixed[pl.ds(pl.multiple_of(32 * f + 8 * k, 8), 8), :]
            top = plane[0:8] + jnp.where(upper, outside, 0.0)
            bottom = plane[rows - 8 : rows] + jnp.where(upper, 0.0, outside)
            late[0, f, k] = top[0:4]
            late[1, f, k] = bottom[4:8]
            plane = jnp.abs(jnp.concatenate([top, plane[8 : rows - 8], bottom], axis=0))
            peak = plane if peak is None else jnp.maximum(peak, plane)
        beside[...] = pltpu.roll(columns_now, LANES - PLANES, 1)
        peak = jnp.maximum(peak, pltpu.roll(peak, 32, 1))
        peak = jnp.maximum(peak, pltpu.roll(peak, 64, 1))
        peak = jnp.maximum(peak, pltpu.roll(peak, rows - 1, 0))
        peak = jnp.maximum(peak, pltpu.roll(peak, rows - 2, 0))
        folded[f, pl.ds(0, rows), :] = peak
        return carry

    lax.fori_loop(0, FIELDS, complete, 0)
    for i, to in ((0, 0), (1, last)):

        @pl.when(t != to)
        def _():
            send(late.at[i], landed.at[t], bulk_send, bulk_recv, (s, to))

        @pl.when(t == to)
        def _():
            pltpu.make_async_copy(late.at[i], landed.at[t], own_sem).start()


    some = pl.ds(0, n_section - 1)
    arrived(member_rows.at[some], member_recv)
    block_rows = member_cols.shape[1]
    for r in range(n_section):
        for col in range(n_section // 4):
            member_cols[col, pl.ds(r, 1), :] = member_rows[r, :, pl.ds(col * LANES, LANES)]
    slots = slot_ref[...].astype(jnp.float32)
    at = lax.broadcasted_iota(jnp.int32, slots.shape, 1)
    slot = jnp.max(jnp.where(at == t, slots, 0.0), axis=1, keepdims=True)
    slot = jnp.broadcast_to(slot, (block_rows, LANES))
    labels = jnp.full((block_rows, LANES), -1, jnp.int32)
    for p in range(n_section):
        window = member_cols[p // 4]
        turned = pltpu.roll(window, LANES - 32 * (p % 4), 1) if p % 4 else window
        labels = jnp.where(slot == float(p), turned, labels)
    peaks = [folded[f, pl.ds(0, block_rows, stride=4), :] for f in range(FIELDS)]
    best[...] = jnp.zeros(best.shape, jnp.float32)
    columns = GROUPS // LANES
    wide = lax.broadcasted_iota(jnp.int32, (block_rows, LANES), 1)

    def collect(j, carry):
        labels, peaks = carry[0], carry[1:]
        label = jnp.broadcast_to(labels[:, 0:1], (block_rows, LANES))
        spread = [jnp.broadcast_to(p[:, 0:1], (block_rows, LANES)) for p in peaks]
        for col in range(columns):
            match = label == wide + LANES * col
            for f in range(FIELDS):
                found = jnp.where(match, spread[f], 0.0)
                top = best[f, col]
                for r in range(block_rows // 8):
                    top = jnp.maximum(top, found[8 * r : 8 * r + 8])
                best[f, col] = top
        return tuple(pltpu.roll(a, LANES - 1, 1) for a in carry)

    lax.fori_loop(0, 32, collect, (labels, *peaks))

    depth = own.shape[1]
    own[...] = jnp.zeros(own.shape, jnp.float32)
    for f in range(FIELDS):
        for col in range(columns):
            at = f * columns + col
            own[at // depth, pl.ds(at % depth, 1), :] = jnp.max(best[f, col], axis=0, keepdims=True)

    for d in range(1, shards):
        other = (place + d) % shards
        send(own.at[other], pass1.at[d - 1], red_send.at[0], red_recv.at[0], in_plane(d))
    arrived(pass1, red_recv.at[0])
    value = own[place]
    for d in range(shards - 1):
        value = jnp.maximum(value, pass1[d])
    if Y_CHIPS > 1:
        hold[0] = value
        for d in range(1, Y_CHIPS):
            send(hold.at[0], pass2.at[d - 1], red_send.at[1], red_recv.at[1], in_column(d))
        arrived(pass2, red_recv.at[1])
        for d in range(Y_CHIPS - 1):
            value = jnp.maximum(value, pass2[d])
    hold[1] = value
    for d in range(1, z_all):
        send(hold.at[1], pass3.at[d - 1], red_send.at[2], red_recv.at[2], in_depth(d))
    deliver(3, 2)
    arrived(pass3, red_recv.at[2])
    for d in range(z_all - 1):
        value = jnp.maximum(value, pass3[d])
    hold[2] = value
    for d in range(1, shards):
        send(hold.at[2], full.at[place], red_send.at[3], red_recv.at[3], in_plane(d))
    full[place] = value
    arrived(full.at[pl.ds(0, shards - 1)], red_recv.at[3])
    for i in range(shards):
        final[pl.ds(i * depth, depth), :] = full[i]

    for copy in halo_copies():
        copy.wait_send()
    arrived(fringe.at[some], fringe_recv)
    arrived(fringe_out.at[some], fringe_send)
    arrived(fringe_out.at[0], fringe_own)
    arrived(member_rows.at[some], member_send)
    arrived(outbox.at[some], bulk_send)
    arrived(pass1, red_send.at[0])
    if Y_CHIPS > 1:
        arrived(pass2, red_send.at[1])
    arrived(pass3, red_send.at[2])
    arrived(pass1, red_send.at[3])
    arrived(landed.at[0], own_sem)
    arrived(landed.at[some], bulk_recv)


def place_kernel(slot_ref, final, members, landed, fringe, coded, group_peak, peaks, scale, beside, added):
    n_section = landed.shape[0]
    columns = GROUPS // LANES

    @pl.when(pl.program_id(0) == 0)
    def _():
        peaks[...] = jnp.zeros(peaks.shape, jnp.float32)
        for f in range(FIELDS):
            for col in range(columns):
                peaks[f : f + 1, col * LANES : (col + 1) * LANES] = final[f * columns + col : f * columns + col + 1, :]
        group_peak[...] = peaks[0:FIELDS, :]
        lane = lax.broadcasted_iota(jnp.int32, (8, LANES), 1)
        for block in range(n_section // 4):
            label = jnp.broadcast_to(members[0:1, block * LANES : (block + 1) * LANES], (8, LANES))
            high, low = label // LANES, label % LANES
            found = jnp.zeros((8, LANES), jnp.float32)
            for col in range(columns):
                picked = jnp.take_along_axis(
                    peaks[:, col * LANES : (col + 1) * LANES], low, axis=1, mode="promise_in_bounds"
                )
                found = jnp.where(high == col, picked, found)
            found = 1.0 / (found + EPSILON)
            turned = [found] + [pltpu.roll(found, 32 * q, 1) for q in range(1, 4)]
            for q in range(4):
                full = turned[(0 - q) % 4]
                for a in range(1, 4):
                    full = jnp.where(lane // 32 == a, turned[(a - q) % 4], full)
                for f in range(FIELDS):
                    scale[f, 4 * block + q] = full[f : f + 1]
        edges = fringe[...].reshape(4 * n_section, LANES)
        side = lax.broadcasted_iota(jnp.int32, edges.shape, 1)
        beside[...] = jnp.where(side < 64, pltpu.roll(edges, 4 * n_section - 4, 0), pltpu.roll(edges, 4, 0))

    f = pl.program_id(0)
    c = cosines()
    edges = beside[...]
    side = lax.broadcasted_iota(jnp.int32, edges.shape, 1)
    first = jnp.zeros(edges.shape, jnp.float32)
    final_cell = jnp.zeros(edges.shape, jnp.float32)
    for k in range(4):
        first = jnp.where(side == 32 * k, float(c[k, 0]), first)
        final_cell = jnp.where(side == 32 * k + 31, float(c[k, 3]), final_cell)
    for k in range(PLANES):
        extra = final_cell * edges[:, k : k + 1] + first * edges[:, 64 + k : 65 + k]
        added[:, k] = extra.reshape(n_section, 4, LANES)
    beside[...] = pltpu.roll(edges, LANES - PLANES, 1)

    for b in range(n_section):
        slot = slot_ref[0, b]
        factor = scale[f, slot]
        coded[0, :, :, pl.ds(pl.multiple_of(slot * LANES, LANES), LANES)] = (landed[b, 0] + added[b]) * factor[None]


def per_device(density, momentum, energy, membership, slot_of_brick):
    planes, rows, width = density.shape
    n_section = rows // 4
    block_rows = -(-n_section // 8) * 8
    shards = CORES * X_CHIPS
    depth = 64 // shards
    f32 = jnp.float32
    height = rows + 2 * EDGE
    vmem, anywhere = pl.BlockSpec(memory_space=pltpu.VMEM), pl.BlockSpec(memory_space=pl.ANY)
    smem = pl.BlockSpec(memory_space=pltpu.SMEM)
    dma = pltpu.SemaphoreType.DMA
    landed, fringe, final = pl.pallas_call(
        step_kernel,
        out_shape=(
            jax.ShapeDtypeStruct((n_section, FIELDS, planes, 4, width), f32),
            jax.ShapeDtypeStruct((n_section, 4, width), f32),
            jax.ShapeDtypeStruct((64, width), f32),
        ),
        in_specs=[vmem, anywhere, anywhere, anywhere, anywhere, vmem, vmem, vmem, vmem],
        out_specs=(anywhere, anywhere, vmem),
        scratch_shapes=[
            pltpu.VMEM((FIELDS, planes, height, width), f32),
            pltpu.VMEM((FIELDS, planes, height, width), f32),
            pltpu.VMEM((FIELDS, planes, height, width), f32),
            pltpu.VMEM((FIELDS, planes, height, width), f32),
            pltpu.VMEM((n_section, FIELDS, planes, 4, width), f32),
            pltpu.VMEM((2, FIELDS, planes, 4, width), f32),
            pltpu.VMEM((height, width), f32),
            pltpu.VMEM((FIELDS, planes, rows, width), f32),
            pltpu.VMEM((rows, width), f32),
            pltpu.VMEM((FIELDS * 32, width), f32),
            pltpu.VMEM((n_section, 4, width), f32),
            pltpu.VMEM((FIELDS, 4 * block_rows, width), f32),
            pltpu.VMEM((n_section, 1, membership.shape[1]), jnp.int32),
            pltpu.VMEM((n_section // 4, block_rows, width), jnp.int32),
            pltpu.VMEM((2, FIELDS, 8, width), f32),
            pltpu.VMEM((2, 3, FIELDS, 8, width), f32),
            pltpu.VMEM((2, 3, FIELDS, 8, width), f32),
            pltpu.VMEM((FIELDS, GROUPS // width, 8, width), f32),
            pltpu.VMEM((shards, depth, width), f32),
            pltpu.VMEM((shards - 1, depth, width), f32),
            pltpu.VMEM((max(Y_CHIPS - 1, 1), depth, width), f32),
            pltpu.VMEM((Z_HI * Z_LO - 1, depth, width), f32),
            pltpu.VMEM((3, depth, width), f32),
            pltpu.VMEM((shards, depth, width), f32),
            dma((4,)),
            dma((2, 3)),
            dma((2, 3)),
            dma((2, 3)),
            dma((2, 3)),
            dma,
            dma,
            dma,
            dma,
            dma,
            dma,
            dma,
            dma,
            dma((4,)),
            dma((4,)),
        ],
        compiler_params=pltpu.CompilerParams(collective_id=0, has_side_effects=True),
        name="step",
    )(slot_of_brick, density, momentum, energy, membership, row_matrix(rows), brick_matrix(), depth_matrix(), outer_matrix(rows))
    return pl.pallas_call(
        place_kernel,
        grid=(FIELDS,),
        out_shape=(
            jax.ShapeDtypeStruct((FIELDS, planes, 4, n_section * width), f32),
            jax.ShapeDtypeStruct((FIELDS, GROUPS), f32),
        ),
        in_specs=[
            smem,
            pl.BlockSpec((64, width), lambda f: (0, 0)),
            pl.BlockSpec(membership.shape, lambda f: (0, 0)),
            pl.BlockSpec((n_section, 1, planes, 4, width), lambda f: (0, f, 0, 0, 0)),
            pl.BlockSpec((n_section, 4, width), lambda f: (0, 0, 0)),
        ],
        out_specs=(
            pl.BlockSpec((1, planes, 4, n_section * width), lambda f: (f, 0, 0, 0)),
            pl.BlockSpec((FIELDS, GROUPS), lambda f: (0, 0)),
        ),
        scratch_shapes=[
            pltpu.VMEM((8, GROUPS), f32),
            pltpu.VMEM((FIELDS, n_section, 1, width), f32),
            pltpu.VMEM((rows, width), f32),
            pltpu.VMEM((n_section, planes, 4, width), f32),
        ],
        name="place",
    )(slot_of_brick, final, membership, landed, fringe)


def solution(mesh):
    placed = (
        P(None, "sim", "section"),
        P(None, None, "sim", "section"),
        P(None, "sim", "section"),
        P(("sim", "section"), None),
        P("sim", None),
    )
    return jax.shard_map(
        per_device,
        mesh=mesh,
        in_specs=placed,
        out_specs=(P(None, None, ("sim", "section"), None), P()),
        check_vma=False,
    )
```

```python
import functools

import jax
import jax.numpy as jnp
import numpy as np
from jax import lax
from jax.experimental import pallas as pl
from jax.experimental.pallas import tpu as pltpu
from jax.sharding import PartitionSpec as P

Z_HI, Y_CHIPS, CORES = 2, 8, 2
X_CHIPS, Z_LO = 4, 6
GAMMA_LESS, COURANT, DIFFUSE, EPSILON = 0.4, 0.05, 0.1, 1e-06
FIELDS, PLANES, LANES, EDGE = 5, 4, 128, 8
GROUPS = 1536
HIGH = lax.Precision.HIGHEST
MESH = pl.DeviceIdType.MESH


def cosines():
    k = np.arange(4)[:, None]
    m = np.arange(4)[None, :]
    return np.where(k == 0, 0.5, np.sqrt(0.5)) * np.cos(np.pi * (2 * m + 1) * k / 8)


def row_matrix(rows):
    predict = np.zeros((rows, rows + 2 * EDGE))
    for y in range(rows):
        at = y + EDGE
        predict[y, at] = 1.0
        predict[y, [at - 1, at + 1]] = -9.0 / 16.0
        predict[y, [at - 3, at + 3]] = 1.0 / 16.0
    return (np.kron(np.eye(rows // 4), cosines()) @ predict).astype(np.float32)


def outer_matrix(rows):
    whole = row_matrix(rows)
    out = np.zeros((8, 32), np.float32)
    out[:4, :16] = whole[:4, :16]
    out[4:, 16:] = whole[rows - 4 :, rows:]
    return out


def brick_matrix():
    c = cosines()
    out = np.zeros((LANES, LANES))
    for j in range(LANES // 4):
        for k in range(4):
            out[4 * j : 4 * j + 4, k * (LANES // 4) + j] = c[k]
    return out.astype(np.float32)


def depth_matrix():
    return np.kron(np.eye(LANES // 4), cosines().T).astype(np.float32)


def state_terms(c):
    rho, mx, my, mz, energy = c
    inverse = 1.0 / rho
    u = mx * inverse
    v = my * inverse
    pressure = GAMMA_LESS * (energy - 0.5 * (mx * mx + my * my + mz * mz) * inverse)
    total = energy + pressure
    flux_x = (mx, mx * u + pressure, my * u, mz * u, total * u)
    flux_y = (my, mx * v, my * v + pressure, mz * v, total * v)
    spread = [DIFFUSE * a for a in c]
    return (
        [b - COURANT * a for a, b in zip(flux_x, spread)],
        [b + COURANT * a for a, b in zip(flux_x, spread)],
        [b - COURANT * a for a, b in zip(flux_y, spread)],
        [b + COURANT * a for a, b in zip(flux_y, spread)],
    )


def step_kernel(
    slot_ref,
    density,
    momentum,
    energy,
    members,
    rows_ref,
    brick_ref,
    depth_ref,
    outer_ref,
    landed,
    fringe,
    final,
    ext,
    center,
    from_above,
    from_below,
    outbox,
    late,
    edge_rows,
    planes_done,
    beside,
    beyond_mixed,
    fringe_out,
    folded,
    member_rows,
    member_cols,
    edge_out,
    edge_in,
    edge_term,
    best,
    own,
    pass1,
    pass2,
    pass3,
    hold,
    full,
    load_sem,
    row_send,
    row_recv,
    edge_send,
    edge_recv,
    member_send,
    member_recv,
    bulk_send,
    bulk_recv,
    own_sem,
    fringe_send,
    fringe_recv,
    fringe_own,
    red_send,
    red_recv,
):
    n_section = X_CHIPS * Z_LO
    n_sim = Z_HI * Y_CHIPS * CORES
    rows = 4 * n_section
    tiles = rows // 8
    s = lax.axis_index("sim")
    t = lax.axis_index("section")
    core = s % CORES
    y = (s // CORES) % Y_CHIPS
    z_hi = s // (CORES * Y_CHIPS)
    x = t // Z_LO
    z_lo = t % Z_LO
    below, above = (s + n_sim - 1) % n_sim, (s + 1) % n_sim
    left, right = (t + n_section - 1) % n_section, (t + 1) % n_section
    lane = lax.broadcasted_iota(jnp.int32, (8, LANES), 1)

    loads = [
        pltpu.make_async_copy(density, ext.at[0, :, pl.ds(EDGE, rows), :], load_sem.at[0]),
        pltpu.make_async_copy(momentum, ext.at[pl.ds(1, 3), :, pl.ds(EDGE, rows), :], load_sem.at[1]),
        pltpu.make_async_copy(energy, ext.at[4, :, pl.ds(EDGE, rows), :], load_sem.at[2]),
        pltpu.make_async_copy(members, member_rows.at[t], load_sem.at[3]),
    ]
    for copy in loads:
        copy.start()

    barrier = pltpu.get_barrier_semaphore()
    shards = CORES * Y_CHIPS
    place = core * Y_CHIPS + y
    z_all = Z_HI * Z_LO
    z = z_hi * Z_LO + z_lo

    def in_plane(step):
        other = (place + step) % shards
        return (z_hi * (CORES * Y_CHIPS) + (other % Y_CHIPS) * CORES + other // Y_CHIPS, t)

    def in_column(step):
        return (s, ((x + step) % X_CHIPS) * Z_LO + z_lo)

    def in_depth(step):
        other = (z + step) % z_all
        return (s + (other // Z_LO - z_hi) * (CORES * Y_CHIPS), x * Z_LO + other % Z_LO)

    def greet(device):
        pl.semaphore_signal(barrier, inc=1, device_id=device, device_id_type=MESH)

    def greet_section(d, carry):
        greet((s, (t + d) % n_section))
        return carry

    lax.fori_loop(1, n_section, greet_section, 0)
    for sim in (below, above):
        for section in (left, t, right):
            greet((sim, section))
    for d in range(1, shards):
        greet(in_plane(d))
    if Z_HI > 1:
        for d in range(Z_LO):
            greet(((s + n_sim // 2) % n_sim, x * Z_LO + d))
    greetings = (n_section - 1) + 6 + (shards - 1) + (Z_LO if Z_HI > 1 else 0)

    for copy in loads:
        copy.wait()

    def pack(f, carry):
        low = jnp.zeros((8, LANES), jnp.float32)
        high = jnp.zeros((8, LANES), jnp.float32)
        for plane in range(PLANES):
            for r in range(tiles):
                value = ext[f, plane, pl.ds(EDGE + 8 * r, 8), :]
                at = 4 * r + plane
                low = jnp.where(lane == at, pltpu.roll(value, at, 1) if at else value, low)
                high = jnp.where(lane == at, pltpu.roll(value, at + 1, 1), high)
        edge_out[0, f] = low
        edge_out[1, f] = high
        return carry

    lax.fori_loop(0, FIELDS, pack, 0)

    def cells(plane, r):
        start = pl.multiple_of(8 * r, 8) if not isinstance(r, int) else 8 * r
        c = [ext[f, plane, pl.ds(start, 8), :] for f in range(FIELDS)]
        low_x, high_x, low_y, high_y = state_terms(c)
        for f in range(FIELDS):
            up = jnp.where(lane == LANES - 1, 0.0, pltpu.roll(low_x[f], LANES - 1, 1))
            down = jnp.where(lane == 0, 0.0, pltpu.roll(high_x[f], 1, 1))
            center[f, plane, pl.ds(start, 8), :] = (1.0 - 4.0 * DIFFUSE) * c[f] + up + down
            from_above[f, plane, pl.ds(start, 8), :] = low_y[f]
            from_below[f, plane, pl.ds(start, 8), :] = high_y[f]
        return low_x, high_x

    nothing = jnp.zeros((8, LANES), jnp.float32)
    height = rows + 2 * EDGE
    for first in (0, height - 8):
        edge_rows[pl.ds(first, 8), :] = nothing
        for f in range(FIELDS):
            for plane in range(PLANES):
                for ref in (center, from_above, from_below):
                    ref[f, plane, pl.ds(first, 8), :] = nothing

    def inner(r, carry):
        packed = nothing
        for plane in range(PLANES):
            low_x, high_x = cells(plane, r)
            for f in range(FIELDS):
                at = PLANES * f + plane
                packed = jnp.where(lane == at, pltpu.roll(low_x[f], at, 1) if at else low_x[f], packed)
                packed = jnp.where(lane == 64 + at, pltpu.roll(high_x[f], 65 + at, 1), packed)
        edge_rows[pl.ds(pl.multiple_of(8 * r, 8), 8), :] = packed
        return carry

    lax.fori_loop(1, tiles + 1, inner, 0)

    def product(a, b):
        return jnp.dot(a, b, precision=HIGH, preferred_element_type=jnp.float32)

    edges_done = product(product(rows_ref[...], edge_rows[...]), depth_ref[...])
    fringe_out[...] = edges_done.reshape(n_section, 4, LANES)
    for first in (0, n_section - 1):
        fringe_out[first] = jnp.zeros((4, LANES), jnp.float32)

    def send(source, target, send_sem, recv_sem, device):
        copy = pltpu.make_async_remote_copy(
            src_ref=source, dst_ref=target, send_sem=send_sem, recv_sem=recv_sem, device_id=device, device_id_type=MESH
        )
        copy.start()

    def arrived(ref, sem):
        pltpu.make_async_copy(ref, ref, sem).wait()

    def halo_copies():
        plan = []
        for side, step in ((0, left), (1, right)):
            for k, sim in ((0, above), (1, s), (2, below)):
                plan.append((edge_out.at[side], edge_in.at[1 - side, k], edge_send.at[side, k], edge_recv.at[1 - side, k], (sim, step)))
        for i, (first, to, sim) in enumerate(((0, EDGE + rows, below), (rows - 8, 0, above))):
            plan.append((density.at[:, pl.ds(first, 8), :], ext.at[0, :, pl.ds(to, 8), :], row_send.at[i, 0], row_recv.at[i, 0], (sim, t)))
            plan.append((momentum.at[:, :, pl.ds(first, 8), :], ext.at[pl.ds(1, 3), :, pl.ds(to, 8), :], row_send.at[i, 1], row_recv.at[i, 1], (sim, t)))
            plan.append((energy.at[:, pl.ds(first, 8), :], ext.at[4, :, pl.ds(to, 8), :], row_send.at[i, 2], row_recv.at[i, 2], (sim, t)))
        return [
            pltpu.make_async_remote_copy(
                src_ref=a, dst_ref=b, send_sem=c, recv_sem=d, device_id=e, device_id_type=MESH
            )
            for a, b, c, d, e in plan
        ]

    c = cosines()
    a1, b1 = float(c[1, 0]), float(c[1, 1])

    def mix(parts):
        outer_sum, inner_sum = parts[0] + parts[3], parts[1] + parts[2]
        outer_gap, inner_gap = parts[0] - parts[3], parts[1] - parts[2]
        return jnp.concatenate(
            [
                0.5 * (outer_sum + inner_sum),
                a1 * outer_gap + b1 * inner_gap,
                0.5 * (outer_sum - inner_sum),
                b1 * outer_gap - a1 * inner_gap,
            ],
            axis=0,
        )

    def transformed(f):
        parts = []
        for plane in range(PLANES):
            updated = center[f, plane] + pltpu.roll(from_above[f, plane], height - 1, 0)
            updated += pltpu.roll(from_below[f, plane], 1, 0)
            parts.append(product(rows_ref[...], updated))
        done = product(mix(parts), brick_ref[...])
        return [done[k * rows : (k + 1) * rows] for k in range(PLANES)]

    last = n_section - 1
    is_inside = jnp.logical_and(t > 0, t < last)

    def deliver(first, count):
        some_fields = pl.ds(first, count)

        def visit(d, carry):
            to = 1 + (t + d) % (n_section - 2)

            @pl.when(to != t)
            def _():
                send(outbox.at[to, some_fields], landed.at[t, some_fields], bulk_send, bulk_recv, (s, to))

            return carry

        lax.fori_loop(0, n_section - 2, visit, 0)

        @pl.when(is_inside)
        def _():
            pltpu.make_async_copy(outbox.at[t, some_fields], landed.at[t, some_fields], own_sem).start()

    def early(f, carry):
        for k, plane in enumerate(transformed(f)):
            outbox[:, f, k] = plane.reshape(n_section, 4, LANES)
            planes_done[f, k] = plane

        @pl.when(f == 0)
        def _():
            pl.semaphore_wait(barrier, greetings)
            for copy in halo_copies():
                copy.start()

            def send_small(d, carry):
                to = (t + d) % n_section
                send(members, member_rows.at[t], member_send, member_recv, (s, to))
                send(fringe_out.at[to], fringe.at[t], fringe_send, fringe_recv, (s, to))
                return carry

            lax.fori_loop(1, n_section, send_small, 0)
            pltpu.make_async_copy(fringe_out.at[t], fringe.at[t], fringe_own).start()

        @pl.when(f == 2)
        def _():
            deliver(0, 3)

        return carry

    lax.fori_loop(0, FIELDS, early, 0)

    for copy in halo_copies():
        copy.wait_recv()

    def edges(k, carry):
        for side in range(2):
            terms = state_terms([edge_in[side, k, f] for f in range(FIELDS)])[1 - side]
            for f in range(FIELDS):
                edge_term[side, k, f] = terms[f]
        return carry

    lax.fori_loop(0, 3, edges, 0)

    def outer(plane, carry):
        cells(plane, 0)
        cells(plane, tiles + 1)
        return carry

    lax.fori_loop(0, PLANES, outer, 0)

    group = lane // PLANES
    for r in range(tiles + 2):
        k = 0 if r == 0 else 2 if r == tiles + 1 else 1
        at = (r - 1) % tiles
        packed = nothing
        for f in range(FIELDS):
            packed = jnp.where(group == f, pltpu.roll(edge_term[1, k, f], (4 * (f - at)) % LANES, 1), packed)
            packed = jnp.where(group == 16 + f, pltpu.roll(edge_term[0, k, f], (64 + 4 * (f - at)) % LANES, 1), packed)
        edge_rows[pl.ds(8 * r, 8), :] = packed
    beside[...] = product(product(rows_ref[...], edge_rows[...]), depth_ref[...])

    def beyond(f, carry):
        parts = []
        for plane in range(PLANES):
            halves = []
            for first, low in ((0, True), (height - 8, False)):
                tile = [ref[f, plane, pl.ds(first, 8), :] for ref in (center, from_above, from_below)]
                both = [jnp.concatenate([a, nothing] if low else [nothing, a], axis=0) for a in tile]
                halves.append(both[0] + pltpu.roll(both[1], 15, 0) + pltpu.roll(both[2], 1, 0))
            parts.append(jnp.concatenate(halves, axis=0))
        made = product(outer_ref[...], jnp.concatenate(parts, axis=1))
        beyond_mixed[pl.ds(pl.multiple_of(32 * f, 32), 32), :] = mix(
            [made[:, LANES * k : LANES * (k + 1)] for k in range(PLANES)]
        )
        return carry

    lax.fori_loop(0, FIELDS, beyond, 0)
    beyond_mixed[...] = product(beyond_mixed[...], brick_ref[...])

    wide_lane = lax.broadcasted_iota(jnp.int32, (rows, LANES), 1)
    first_cell = jnp.zeros((rows, LANES), jnp.float32)
    final_cell = jnp.zeros((rows, LANES), jnp.float32)
    for k in range(4):
        first_cell = jnp.where(wide_lane == 32 * k, float(c[k, 0]), first_cell)
        final_cell = jnp.where(wide_lane == 32 * k + 31, float(c[k, 3]), final_cell)
    upper = lax.broadcasted_iota(jnp.int32, (8, LANES), 0) < 4

    def complete(f, carry):
        peak = None
        columns_now = beside[...]
        for k in range(PLANES):
            plane = planes_done[f, k] + final_cell * columns_now[:, k : k + 1] + first_cell * columns_now[:, 64 + k : 65 + k]
            outside = beyond_mixed[pl.ds(pl.multiple_of(32 * f + 8 * k, 8), 8), :]
            top = plane[0:8] + jnp.where(upper, outside, 0.0)
            bottom = plane[rows - 8 : rows] + jnp.where(upper, 0.0, outside)
            late[0, f, k] = top[0:4]
            late[1, f, k] = bottom[4:8]
            plane = jnp.abs(jnp.concatenate([top, plane[8 : rows - 8], bottom], axis=0))
            peak = plane if peak is None else jnp.maximum(peak, plane)
        beside[...] = pltpu.roll(columns_now, LANES - PLANES, 1)
        peak = jnp.maximum(peak, pltpu.roll(peak, 32, 1))
        peak = jnp.maximum(peak, pltpu.roll(peak, 64, 1))
        peak = jnp.maximum(peak, pltpu.roll(peak, rows - 1, 0))
        peak = jnp.maximum(peak, pltpu.roll(peak, rows - 2, 0))
        folded[f, pl.ds(0, rows), :] = peak
        return carry

    lax.fori_loop(0, FIELDS, complete, 0)
    for i, to in ((0, 0), (1, last)):

        @pl.when(t != to)
        def _():
            send(late.at[i], landed.at[t], bulk_send, bulk_recv, (s, to))

        @pl.when(t == to)
        def _():
            pltpu.make_async_copy(late.at[i], landed.at[t], own_sem).start()


    some = pl.ds(0, n_section - 1)
    arrived(member_rows.at[some], member_recv)
    block_rows = member_cols.shape[1]
    for r in range(n_section):
        for col in range(n_section // 4):
            member_cols[col, pl.ds(r, 1), :] = member_rows[r, :, pl.ds(col * LANES, LANES)]
    slots = slot_ref[...].astype(jnp.float32)
    at = lax.broadcasted_iota(jnp.int32, slots.shape, 1)
    slot = jnp.max(jnp.where(at == t, slots, 0.0), axis=1, keepdims=True)
    slot = jnp.broadcast_to(slot, (block_rows, LANES))
    labels = jnp.full((block_rows, LANES), -1, jnp.int32)
    for p in range(n_section):
        window = member_cols[p // 4]
        turned = pltpu.roll(window, LANES - 32 * (p % 4), 1) if p % 4 else window
        labels = jnp.where(slot == float(p), turned, labels)
    peaks = [folded[f, pl.ds(0, block_rows, stride=4), :] for f in range(FIELDS)]
    best[...] = jnp.zeros(best.shape, jnp.float32)
    columns = GROUPS // LANES
    wide = lax.broadcasted_iota(jnp.int32, (block_rows, LANES), 1)

    def collect(j, carry):
        labels, peaks = carry[0], carry[1:]
        label = jnp.broadcast_to(labels[:, 0:1], (block_rows, LANES))
        spread = [jnp.broadcast_to(p[:, 0:1], (block_rows, LANES)) for p in peaks]
        for col in range(columns):
            match = label == wide + LANES * col
            for f in range(FIELDS):
                found = jnp.where(match, spread[f], 0.0)
                top = best[f, col]
                for r in range(block_rows // 8):
                    top = jnp.maximum(top, found[8 * r : 8 * r + 8])
                best[f, col] = top
        return tuple(pltpu.roll(a, LANES - 1, 1) for a in carry)

    lax.fori_loop(0, 32, collect, (labels, *peaks))

    depth = own.shape[1]
    own[...] = jnp.zeros(own.shape, jnp.float32)
    for f in range(FIELDS):
        for col in range(columns):
            at = f * columns + col
            own[at // depth, pl.ds(at % depth, 1), :] = jnp.max(best[f, col], axis=0, keepdims=True)

    for d in range(1, shards):
        other = (place + d) % shards
        send(own.at[other], pass1.at[d - 1], red_send.at[0], red_recv.at[0], in_plane(d))
    arrived(pass1, red_recv.at[0])
    value = own[place]
    for d in range(shards - 1):
        value = jnp.maximum(value, pass1[d])
    if X_CHIPS > 1:
        hold[0] = value
        for d in range(1, X_CHIPS):
            send(hold.at[0], pass2.at[d - 1], red_send.at[1], red_recv.at[1], in_column(d))
        arrived(pass2, red_recv.at[1])
        for d in range(X_CHIPS - 1):
            value = jnp.maximum(value, pass2[d])
    hold[1] = value
    for d in range(1, z_all):
        send(hold.at[1], pass3.at[d - 1], red_send.at[2], red_recv.at[2], in_depth(d))
    deliver(3, 2)
    arrived(pass3, red_recv.at[2])
    for d in range(z_all - 1):
        value = jnp.maximum(value, pass3[d])
    hold[2] = value
    for d in range(1, shards):
        send(hold.at[2], full.at[place], red_send.at[3], red_recv.at[3], in_plane(d))
    full[place] = value
    arrived(full.at[pl.ds(0, shards - 1)], red_recv.at[3])
    for i in range(shards):
        final[pl.ds(i * depth, depth), :] = full[i]

    for copy in halo_copies():
        copy.wait_send()
    arrived(fringe.at[some], fringe_recv)
    arrived(fringe_out.at[some], fringe_send)
    arrived(fringe_out.at[0], fringe_own)
    arrived(member_rows.at[some], member_send)
    arrived(outbox.at[some], bulk_send)
    arrived(pass1, red_send.at[0])
    if X_CHIPS > 1:
        arrived(pass2, red_send.at[1])
    arrived(pass3, red_send.at[2])
    arrived(pass1, red_send.at[3])
    arrived(landed.at[0], own_sem)
    arrived(landed.at[some], bulk_recv)


def place_kernel(slot_ref, final, members, landed, fringe, coded, group_peak, peaks, scale, added):
    n_section = landed.shape[0]
    columns = GROUPS // LANES

    peaks[...] = jnp.zeros(peaks.shape, jnp.float32)
    for f in range(FIELDS):
        for col in range(columns):
            peaks[f : f + 1, col * LANES : (col + 1) * LANES] = final[f * columns + col : f * columns + col + 1, :]
    group_peak[...] = peaks[0:FIELDS, :]
    lane = lax.broadcasted_iota(jnp.int32, (8, LANES), 1)
    for block in range(n_section // 4):
        label = jnp.broadcast_to(members[0:1, block * LANES : (block + 1) * LANES], (8, LANES))
        high, low = label // LANES, label % LANES
        found = jnp.zeros((8, LANES), jnp.float32)
        for col in range(columns):
            picked = jnp.take_along_axis(
                peaks[:, col * LANES : (col + 1) * LANES], low, axis=1, mode="promise_in_bounds"
            )
            found = jnp.where(high == col, picked, found)
        found = 1.0 / (found + EPSILON)
        turned = [found] + [pltpu.roll(found, 32 * q, 1) for q in range(1, 4)]
        for q in range(4):
            full = turned[(0 - q) % 4]
            for a in range(1, 4):
                full = jnp.where(lane // 32 == a, turned[(a - q) % 4], full)
            for f in range(FIELDS):
                scale[f, 4 * block + q] = full[f : f + 1]
    edges = fringe[...].reshape(4 * n_section, LANES)
    side = lax.broadcasted_iota(jnp.int32, edges.shape, 1)
    edges = jnp.where(side < 64, pltpu.roll(edges, 4 * n_section - 4, 0), pltpu.roll(edges, 4, 0))

    c = cosines()
    first = jnp.zeros(edges.shape, jnp.float32)
    final_cell = jnp.zeros(edges.shape, jnp.float32)
    for k in range(4):
        first = jnp.where(side == 32 * k, float(c[k, 0]), first)
        final_cell = jnp.where(side == 32 * k + 31, float(c[k, 3]), final_cell)
    for f in range(FIELDS):
        for k in range(PLANES):
            at = PLANES * f + k
            extra = final_cell * edges[:, at : at + 1] + first * edges[:, 64 + at : 65 + at]
            added[:, f, k] = extra.reshape(n_section, 4, LANES)

    def visit(b, carry):
        slot = slot_ref[0, b]
        columns_now = pl.ds(pl.multiple_of(slot * LANES, LANES), LANES)
        for f in range(FIELDS):
            coded[f, :, :, columns_now] = (landed[b, f] + added[b, f]) * scale[f, slot][None]
        return carry

    lax.fori_loop(0, n_section, visit, 0, unroll=4)


def per_device(density, momentum, energy, membership, slot_of_brick):
    planes, rows, width = density.shape
    n_section = rows // 4
    block_rows = -(-n_section // 8) * 8
    shards = CORES * Y_CHIPS
    depth = 64 // shards
    f32 = jnp.float32
    height = rows + 2 * EDGE
    vmem, anywhere = pl.BlockSpec(memory_space=pltpu.VMEM), pl.BlockSpec(memory_space=pl.ANY)
    smem = pl.BlockSpec(memory_space=pltpu.SMEM)
    dma = pltpu.SemaphoreType.DMA
    landed, fringe, final = pl.pallas_call(
        step_kernel,
        out_shape=(
            jax.ShapeDtypeStruct((n_section, FIELDS, planes, 4, width), f32),
            jax.ShapeDtypeStruct((n_section, 4, width), f32),
            jax.ShapeDtypeStruct((64, width), f32),
        ),
        in_specs=[vmem, anywhere, anywhere, anywhere, anywhere, vmem, vmem, vmem, vmem],
        out_specs=(anywhere, anywhere, vmem),
        scratch_shapes=[
            pltpu.VMEM((FIELDS, planes, height, width), f32),
            pltpu.VMEM((FIELDS, planes, height, width), f32),
            pltpu.VMEM((FIELDS, planes, height, width), f32),
            pltpu.VMEM((FIELDS, planes, height, width), f32),
            pltpu.VMEM((n_section, FIELDS, planes, 4, width), f32),
            pltpu.VMEM((2, FIELDS, planes, 4, width), f32),
            pltpu.VMEM((height, width), f32),
            pltpu.VMEM((FIELDS, planes, rows, width), f32),
            pltpu.VMEM((rows, width), f32),
            pltpu.VMEM((FIELDS * 32, width), f32),
            pltpu.VMEM((n_section, 4, width), f32),
            pltpu.VMEM((FIELDS, 4 * block_rows, width), f32),
            pltpu.VMEM((n_section, 1, membership.shape[1]), jnp.int32),
            pltpu.VMEM((n_section // 4, block_rows, width), jnp.int32),
            pltpu.VMEM((2, FIELDS, 8, width), f32),
            pltpu.VMEM((2, 3, FIELDS, 8, width), f32),
            pltpu.VMEM((2, 3, FIELDS, 8, width), f32),
            pltpu.VMEM((FIELDS, GROUPS // width, 8, width), f32),
            pltpu.VMEM((shards, depth, width), f32),
            pltpu.VMEM((shards - 1, depth, width), f32),
            pltpu.VMEM((max(X_CHIPS - 1, 1), depth, width), f32),
            pltpu.VMEM((Z_HI * Z_LO - 1, depth, width), f32),
            pltpu.VMEM((3, depth, width), f32),
            pltpu.VMEM((shards, depth, width), f32),
            dma((4,)),
            dma((2, 3)),
            dma((2, 3)),
            dma((2, 3)),
            dma((2, 3)),
            dma,
            dma,
            dma,
            dma,
            dma,
            dma,
            dma,
            dma,
            dma((4,)),
            dma((4,)),
        ],
        compiler_params=pltpu.CompilerParams(collective_id=0, has_side_effects=True),
        name="step",
    )(slot_of_brick, density, momentum, energy, membership, row_matrix(rows), brick_matrix(), depth_matrix(), outer_matrix(rows))
    return pl.pallas_call(
        place_kernel,
        out_shape=(
            jax.ShapeDtypeStruct((FIELDS, planes, 4, n_section * width), f32),
            jax.ShapeDtypeStruct((FIELDS, GROUPS), f32),
        ),
        in_specs=[smem, vmem, vmem, vmem, vmem],
        out_specs=(vmem, vmem),
        scratch_shapes=[
            pltpu.VMEM((8, GROUPS), f32),
            pltpu.VMEM((FIELDS, n_section, 1, width), f32),
            pltpu.VMEM((n_section, FIELDS, planes, 4, width), f32),
        ],
        name="place",
    )(slot_of_brick, final, membership, landed, fringe)


def solution(mesh):
    placed = (
        P(None, "sim", "section"),
        P(None, None, "sim", "section"),
        P(None, "sim", "section"),
        P(("sim", "section"), None),
        P("sim", None),
    )
    return jax.shard_map(
        per_device,
        mesh=mesh,
        in_specs=placed,
        out_specs=(P(None, None, ("sim", "section"), None), P()),
        check_vma=False,
    )
```

```python
import functools

import jax
import jax.numpy as jnp
import numpy as np
from jax import lax
from jax.experimental import pallas as pl
from jax.experimental.pallas import tpu as pltpu
from jax.sharding import PartitionSpec as P

Z_HI, Y_CHIPS, CORES = 2, 8, 2
X_CHIPS, Z_LO = 4, 6
GAMMA_LESS, COURANT, DIFFUSE, EPSILON = 0.4, 0.05, 0.1, 1e-06
FIELDS, PLANES, LANES, EDGE = 5, 4, 128, 8
GROUPS = 1536
HIGH = lax.Precision.HIGHEST
MESH = pl.DeviceIdType.MESH


def cosines():
    k = np.arange(4)[:, None]
    m = np.arange(4)[None, :]
    return np.where(k == 0, 0.5, np.sqrt(0.5)) * np.cos(np.pi * (2 * m + 1) * k / 8)


def row_matrix(rows):
    predict = np.zeros((rows, rows + 2 * EDGE))
    for y in range(rows):
        at = y + EDGE
        predict[y, at] = 1.0
        predict[y, [at - 1, at + 1]] = -9.0 / 16.0
        predict[y, [at - 3, at + 3]] = 1.0 / 16.0
    return (np.kron(np.eye(rows // 4), cosines()) @ predict).astype(np.float32)


def outer_matrix(rows):
    whole = row_matrix(rows)
    out = np.zeros((8, 32), np.float32)
    out[:4, :16] = whole[:4, :16]
    out[4:, 16:] = whole[rows - 4 :, rows:]
    return out


def brick_matrix():
    c = cosines()
    out = np.zeros((LANES, LANES))
    for j in range(LANES // 4):
        for k in range(4):
            out[4 * j : 4 * j + 4, k * (LANES // 4) + j] = c[k]
    return out.astype(np.float32)


def depth_matrix():
    return np.kron(np.eye(LANES // 4), cosines().T).astype(np.float32)


def state_terms(c):
    rho, mx, my, mz, energy = c
    inverse = 1.0 / rho
    u = mx * inverse
    v = my * inverse
    pressure = GAMMA_LESS * (energy - 0.5 * (mx * mx + my * my + mz * mz) * inverse)
    total = energy + pressure
    flux_x = (mx, mx * u + pressure, my * u, mz * u, total * u)
    flux_y = (my, mx * v, my * v + pressure, mz * v, total * v)
    spread = [DIFFUSE * a for a in c]
    return (
        [b - COURANT * a for a, b in zip(flux_x, spread)],
        [b + COURANT * a for a, b in zip(flux_x, spread)],
        [b - COURANT * a for a, b in zip(flux_y, spread)],
        [b + COURANT * a for a, b in zip(flux_y, spread)],
    )


def step_kernel(
    slot_ref,
    density,
    momentum,
    energy,
    members,
    rows_ref,
    brick_ref,
    depth_ref,
    outer_ref,
    landed,
    fringe,
    final,
    ext,
    center,
    from_above,
    from_below,
    outbox,
    late,
    edge_rows,
    planes_done,
    beside,
    beyond_mixed,
    fringe_out,
    folded,
    member_rows,
    member_cols,
    edge_out,
    edge_in,
    edge_term,
    best,
    own,
    pass1,
    pass2,
    pass3,
    hold,
    full,
    load_sem,
    row_send,
    row_recv,
    edge_send,
    edge_recv,
    member_send,
    member_recv,
    bulk_send,
    bulk_recv,
    own_sem,
    fringe_send,
    fringe_recv,
    fringe_own,
    red_send,
    red_recv,
):
    n_section = X_CHIPS * Z_LO
    n_sim = Z_HI * Y_CHIPS * CORES
    rows = 4 * n_section
    tiles = rows // 8
    s = lax.axis_index("sim")
    t = lax.axis_index("section")
    core = s % CORES
    y = (s // CORES) % Y_CHIPS
    z_hi = s // (CORES * Y_CHIPS)
    x = t // Z_LO
    z_lo = t % Z_LO
    below, above = (s + n_sim - 1) % n_sim, (s + 1) % n_sim
    left, right = (t + n_section - 1) % n_section, (t + 1) % n_section
    lane = lax.broadcasted_iota(jnp.int32, (8, LANES), 1)

    loads = [
        pltpu.make_async_copy(density, ext.at[0, :, pl.ds(EDGE, rows), :], load_sem.at[0]),
        pltpu.make_async_copy(momentum, ext.at[pl.ds(1, 3), :, pl.ds(EDGE, rows), :], load_sem.at[1]),
        pltpu.make_async_copy(energy, ext.at[4, :, pl.ds(EDGE, rows), :], load_sem.at[2]),
        pltpu.make_async_copy(members, member_rows.at[t], load_sem.at[3]),
    ]
    for copy in loads:
        copy.start()

    barrier = pltpu.get_barrier_semaphore()
    shards = CORES * Y_CHIPS
    place = core * Y_CHIPS + y
    z_all = Z_HI * Z_LO
    z = z_hi * Z_LO + z_lo

    def in_plane(step):
        other = (place + step) % shards
        return (z_hi * (CORES * Y_CHIPS) + (other % Y_CHIPS) * CORES + other // Y_CHIPS, t)

    def in_column(step):
        return (s, ((x + step) % X_CHIPS) * Z_LO + z_lo)

    def in_depth(step):
        other = (z + step) % z_all
        return (s + (other // Z_LO - z_hi) * (CORES * Y_CHIPS), x * Z_LO + other % Z_LO)

    def greet(device):
        pl.semaphore_signal(barrier, inc=1, device_id=device, device_id_type=MESH)

    def greet_section(d, carry):
        greet((s, (t + d) % n_section))
        return carry

    lax.fori_loop(1, n_section, greet_section, 0)
    for sim in (below, above):
        for section in (left, t, right):
            greet((sim, section))
    for d in range(1, shards):
        greet(in_plane(d))
    if Z_HI > 1:
        for d in range(Z_LO):
            greet(((s + n_sim // 2) % n_sim, x * Z_LO + d))
    greetings = (n_section - 1) + 6 + (shards - 1) + (Z_LO if Z_HI > 1 else 0)

    for copy in loads:
        copy.wait()

    def pack(f, carry):
        low = jnp.zeros((8, LANES), jnp.float32)
        high = jnp.zeros((8, LANES), jnp.float32)
        for plane in range(PLANES):
            for r in range(tiles):
                value = ext[f, plane, pl.ds(EDGE + 8 * r, 8), :]
                at = 4 * r + plane
                low = jnp.where(lane == at, pltpu.roll(value, at, 1) if at else value, low)
                high = jnp.where(lane == at, pltpu.roll(value, at + 1, 1), high)
        edge_out[0, f] = low
        edge_out[1, f] = high
        return carry

    lax.fori_loop(0, FIELDS, pack, 0)

    def cells(plane, r):
        start = pl.multiple_of(8 * r, 8) if not isinstance(r, int) else 8 * r
        c = [ext[f, plane, pl.ds(start, 8), :] for f in range(FIELDS)]
        low_x, high_x, low_y, high_y = state_terms(c)
        for f in range(FIELDS):
            up = jnp.where(lane == LANES - 1, 0.0, pltpu.roll(low_x[f], LANES - 1, 1))
            down = jnp.where(lane == 0, 0.0, pltpu.roll(high_x[f], 1, 1))
            center[f, plane, pl.ds(start, 8), :] = (1.0 - 4.0 * DIFFUSE) * c[f] + up + down
            from_above[f, plane, pl.ds(start, 8), :] = low_y[f]
            from_below[f, plane, pl.ds(start, 8), :] = high_y[f]
        return low_x, high_x

    nothing = jnp.zeros((8, LANES), jnp.float32)
    height = rows + 2 * EDGE
    for first in (0, height - 8):
        edge_rows[pl.ds(first, 8), :] = nothing
        for f in range(FIELDS):
            for plane in range(PLANES):
                for ref in (center, from_above, from_below):
                    ref[f, plane, pl.ds(first, 8), :] = nothing

    def inner(r, carry):
        packed = nothing
        for plane in range(PLANES):
            low_x, high_x = cells(plane, r)
            for f in range(FIELDS):
                at = PLANES * f + plane
                packed = jnp.where(lane == at, pltpu.roll(low_x[f], at, 1) if at else low_x[f], packed)
                packed = jnp.where(lane == 64 + at, pltpu.roll(high_x[f], 65 + at, 1), packed)
        edge_rows[pl.ds(pl.multiple_of(8 * r, 8), 8), :] = packed
        return carry

    lax.fori_loop(1, tiles + 1, inner, 0)

    def product(a, b):
        return jnp.dot(a, b, precision=HIGH, preferred_element_type=jnp.float32)

    edges_done = product(product(rows_ref[...], edge_rows[...]), depth_ref[...])
    fringe_out[...] = edges_done.reshape(n_section, 4, LANES)
    for first in (0, n_section - 1):
        fringe_out[first] = jnp.zeros((4, LANES), jnp.float32)

    def send(source, target, send_sem, recv_sem, device):
        copy = pltpu.make_async_remote_copy(
            src_ref=source, dst_ref=target, send_sem=send_sem, recv_sem=recv_sem, device_id=device, device_id_type=MESH
        )
        copy.start()

    def arrived(ref, sem):
        pltpu.make_async_copy(ref, ref, sem).wait()

    def halo_copies():
        plan = []
        for side, step in ((0, left), (1, right)):
            for k, sim in ((0, above), (1, s), (2, below)):
                plan.append((edge_out.at[side], edge_in.at[1 - side, k], edge_send.at[side, k], edge_recv.at[1 - side, k], (sim, step)))
        for i, (first, to, sim) in enumerate(((0, EDGE + rows, below), (rows - 8, 0, above))):
            plan.append((density.at[:, pl.ds(first, 8), :], ext.at[0, :, pl.ds(to, 8), :], row_send.at[i, 0], row_recv.at[i, 0], (sim, t)))
            plan.append((momentum.at[:, :, pl.ds(first, 8), :], ext.at[pl.ds(1, 3), :, pl.ds(to, 8), :], row_send.at[i, 1], row_recv.at[i, 1], (sim, t)))
            plan.append((energy.at[:, pl.ds(first, 8), :], ext.at[4, :, pl.ds(to, 8), :], row_send.at[i, 2], row_recv.at[i, 2], (sim, t)))
        return [
            pltpu.make_async_remote_copy(
                src_ref=a, dst_ref=b, send_sem=c, recv_sem=d, device_id=e, device_id_type=MESH
            )
            for a, b, c, d, e in plan
        ]

    c = cosines()
    a1, b1 = float(c[1, 0]), float(c[1, 1])

    def mix(parts):
        outer_sum, inner_sum = parts[0] + parts[3], parts[1] + parts[2]
        outer_gap, inner_gap = parts[0] - parts[3], parts[1] - parts[2]
        return jnp.concatenate(
            [
                0.5 * (outer_sum + inner_sum),
                a1 * outer_gap + b1 * inner_gap,
                0.5 * (outer_sum - inner_sum),
                b1 * outer_gap - a1 * inner_gap,
            ],
            axis=0,
        )

    def transformed(f):
        parts = []
        for plane in range(PLANES):
            updated = center[f, plane] + pltpu.roll(from_above[f, plane], height - 1, 0)
            updated += pltpu.roll(from_below[f, plane], 1, 0)
            parts.append(product(rows_ref[...], updated))
        done = product(mix(parts), brick_ref[...])
        return [done[k * rows : (k + 1) * rows] for k in range(PLANES)]

    last = n_section - 1
    is_inside = jnp.logical_and(t > 0, t < last)

    def deliver(first, count):
        some_fields = pl.ds(first, count)

        def visit(d, carry):
            to = 1 + (t + d) % (n_section - 2)

            @pl.when(to != t)
            def _():
                send(outbox.at[to, some_fields], landed.at[t, some_fields], bulk_send, bulk_recv, (s, to))

            return carry

        lax.fori_loop(0, n_section - 2, visit, 0)

        @pl.when(is_inside)
        def _():
            pltpu.make_async_copy(outbox.at[t, some_fields], landed.at[t, some_fields], own_sem).start()

    def early(f, carry):
        for k, plane in enumerate(transformed(f)):
            outbox[:, f, k] = plane.reshape(n_section, 4, LANES)
            planes_done[f, k] = plane

        @pl.when(f == 2)
        def _():
            deliver(0, 3)

        return carry

    pl.semaphore_wait(barrier, greetings)
    for copy in halo_copies():
        copy.start()

    def send_small(d, carry):
        to = (t + d) % n_section
        send(members, member_rows.at[t], member_send, member_recv, (s, to))
        send(fringe_out.at[to], fringe.at[t], fringe_send, fringe_recv, (s, to))
        return carry

    lax.fori_loop(1, n_section, send_small, 0)
    pltpu.make_async_copy(fringe_out.at[t], fringe.at[t], fringe_own).start()

    lax.fori_loop(0, FIELDS, early, 0)

    for copy in halo_copies():
        copy.wait_recv()

    def edges(k, carry):
        for side in range(2):
            terms = state_terms([edge_in[side, k, f] for f in range(FIELDS)])[1 - side]
            for f in range(FIELDS):
                edge_term[side, k, f] = terms[f]
        return carry

    lax.fori_loop(0, 3, edges, 0)

    def outer(plane, carry):
        cells(plane, 0)
        cells(plane, tiles + 1)
        return carry

    lax.fori_loop(0, PLANES, outer, 0)

    group = lane // PLANES
    for r in range(tiles + 2):
        k = 0 if r == 0 else 2 if r == tiles + 1 else 1
        at = (r - 1) % tiles
        packed = nothing
        for f in range(FIELDS):
            packed = jnp.where(group == f, pltpu.roll(edge_term[1, k, f], (4 * (f - at)) % LANES, 1), packed)
            packed = jnp.where(group == 16 + f, pltpu.roll(edge_term[0, k, f], (64 + 4 * (f - at)) % LANES, 1), packed)
        edge_rows[pl.ds(8 * r, 8), :] = packed
    beside[...] = product(product(rows_ref[...], edge_rows[...]), depth_ref[...])

    def beyond(f, carry):
        parts = []
        for plane in range(PLANES):
            halves = []
            for first, low in ((0, True), (height - 8, False)):
                tile = [ref[f, plane, pl.ds(first, 8), :] for ref in (center, from_above, from_below)]
                both = [jnp.concatenate([a, nothing] if low else [nothing, a], axis=0) for a in tile]
                halves.append(both[0] + pltpu.roll(both[1], 15, 0) + pltpu.roll(both[2], 1, 0))
            parts.append(jnp.concatenate(halves, axis=0))
        made = product(outer_ref[...], jnp.concatenate(parts, axis=1))
        beyond_mixed[pl.ds(pl.multiple_of(32 * f, 32), 32), :] = mix(
            [made[:, LANES * k : LANES * (k + 1)] for k in range(PLANES)]
        )
        return carry

    lax.fori_loop(0, FIELDS, beyond, 0)
    beyond_mixed[...] = product(beyond_mixed[...], brick_ref[...])

    wide_lane = lax.broadcasted_iota(jnp.int32, (rows, LANES), 1)
    first_cell = jnp.zeros((rows, LANES), jnp.float32)
    final_cell = jnp.zeros((rows, LANES), jnp.float32)
    for k in range(4):
        first_cell = jnp.where(wide_lane == 32 * k, float(c[k, 0]), first_cell)
        final_cell = jnp.where(wide_lane == 32 * k + 31, float(c[k, 3]), final_cell)
    upper = lax.broadcasted_iota(jnp.int32, (8, LANES), 0) < 4

    def complete(f, carry):
        peak = None
        columns_now = beside[...]
        for k in range(PLANES):
            plane = planes_done[f, k] + final_cell * columns_now[:, k : k + 1] + first_cell * columns_now[:, 64 + k : 65 + k]
            outside = beyond_mixed[pl.ds(pl.multiple_of(32 * f + 8 * k, 8), 8), :]
            top = plane[0:8] + jnp.where(upper, outside, 0.0)
            bottom = plane[rows - 8 : rows] + jnp.where(upper, 0.0, outside)
            late[0, f, k] = top[0:4]
            late[1, f, k] = bottom[4:8]
            plane = jnp.abs(jnp.concatenate([top, plane[8 : rows - 8], bottom], axis=0))
            peak = plane if peak is None else jnp.maximum(peak, plane)
        beside[...] = pltpu.roll(columns_now, LANES - PLANES, 1)
        peak = jnp.maximum(peak, pltpu.roll(peak, 32, 1))
        peak = jnp.maximum(peak, pltpu.roll(peak, 64, 1))
        peak = jnp.maximum(peak, pltpu.roll(peak, rows - 1, 0))
        peak = jnp.maximum(peak, pltpu.roll(peak, rows - 2, 0))
        folded[f, pl.ds(0, rows), :] = peak
        return carry

    lax.fori_loop(0, FIELDS, complete, 0)
    for i, to in ((0, 0), (1, last)):

        @pl.when(t != to)
        def _():
            send(late.at[i], landed.at[t], bulk_send, bulk_recv, (s, to))

        @pl.when(t == to)
        def _():
            pltpu.make_async_copy(late.at[i], landed.at[t], own_sem).start()


    some = pl.ds(0, n_section - 1)
    arrived(member_rows.at[some], member_recv)
    block_rows = member_cols.shape[1]
    for r in range(n_section):
        for col in range(n_section // 4):
            member_cols[col, pl.ds(r, 1), :] = member_rows[r, :, pl.ds(col * LANES, LANES)]
    slots = slot_ref[...].astype(jnp.float32)
    at = lax.broadcasted_iota(jnp.int32, slots.shape, 1)
    slot = jnp.max(jnp.where(at == t, slots, 0.0), axis=1, keepdims=True)
    slot = jnp.broadcast_to(slot, (block_rows, LANES))
    labels = jnp.full((block_rows, LANES), -1, jnp.int32)
    for p in range(n_section):
        window = member_cols[p // 4]
        turned = pltpu.roll(window, LANES - 32 * (p % 4), 1) if p % 4 else window
        labels = jnp.where(slot == float(p), turned, labels)
    peaks = [folded[f, pl.ds(0, block_rows, stride=4), :] for f in range(FIELDS)]
    best[...] = jnp.zeros(best.shape, jnp.float32)
    columns = GROUPS // LANES
    wide = lax.broadcasted_iota(jnp.int32, (block_rows, LANES), 1)

    def collect(j, carry):
        labels, peaks = carry[0], carry[1:]
        label = jnp.broadcast_to(labels[:, 0:1], (block_rows, LANES))
        spread = [jnp.broadcast_to(p[:, 0:1], (block_rows, LANES)) for p in peaks]
        for col in range(columns):
            match = label == wide + LANES * col
            for f in range(FIELDS):
                found = jnp.where(match, spread[f], 0.0)
                top = best[f, col]
                for r in range(block_rows // 8):
                    top = jnp.maximum(top, found[8 * r : 8 * r + 8])
                best[f, col] = top
        return tuple(pltpu.roll(a, LANES - 1, 1) for a in carry)

    lax.fori_loop(0, 32, collect, (labels, *peaks), unroll=2)

    depth = own.shape[1]
    own[...] = jnp.zeros(own.shape, jnp.float32)
    for f in range(FIELDS):
        for col in range(columns):
            at = f * columns + col
            own[at // depth, pl.ds(at % depth, 1), :] = jnp.max(best[f, col], axis=0, keepdims=True)

    for d in range(1, shards):
        other = (place + d) % shards
        send(own.at[other], pass1.at[d - 1], red_send.at[0], red_recv.at[0], in_plane(d))
    arrived(pass1, red_recv.at[0])
    value = own[place]
    for d in range(shards - 1):
        value = jnp.maximum(value, pass1[d])
    if X_CHIPS > 1:
        hold[0] = value
        for d in range(1, X_CHIPS):
            send(hold.at[0], pass2.at[d - 1], red_send.at[1], red_recv.at[1], in_column(d))
        arrived(pass2, red_recv.at[1])
        for d in range(X_CHIPS - 1):
            value = jnp.maximum(value, pass2[d])
    hold[1] = value
    for d in range(1, z_all):
        send(hold.at[1], pass3.at[d - 1], red_send.at[2], red_recv.at[2], in_depth(d))
    deliver(3, 2)
    arrived(pass3, red_recv.at[2])
    for d in range(z_all - 1):
        value = jnp.maximum(value, pass3[d])
    hold[2] = value
    for d in range(1, shards):
        send(hold.at[2], full.at[place], red_send.at[3], red_recv.at[3], in_plane(d))
    full[place] = value
    arrived(full.at[pl.ds(0, shards - 1)], red_recv.at[3])
    for i in range(shards):
        final[pl.ds(i * depth, depth), :] = full[i]

    for copy in halo_copies():
        copy.wait_send()
    arrived(fringe.at[some], fringe_recv)
    arrived(fringe_out.at[some], fringe_send)
    arrived(fringe_out.at[0], fringe_own)
    arrived(member_rows.at[some], member_send)
    arrived(outbox.at[some], bulk_send)
    arrived(pass1, red_send.at[0])
    if X_CHIPS > 1:
        arrived(pass2, red_send.at[1])
    arrived(pass3, red_send.at[2])
    arrived(pass1, red_send.at[3])
    arrived(landed.at[0], own_sem)
    arrived(landed.at[some], bulk_recv)


def place_kernel(slot_ref, final, members, landed, fringe, coded, group_peak, peaks, scale, added):
    n_section = landed.shape[0]
    columns = GROUPS // LANES

    peaks[...] = jnp.zeros(peaks.shape, jnp.float32)
    for f in range(FIELDS):
        for col in range(columns):
            peaks[f : f + 1, col * LANES : (col + 1) * LANES] = final[f * columns + col : f * columns + col + 1, :]
    group_peak[...] = peaks[0:FIELDS, :]
    lane = lax.broadcasted_iota(jnp.int32, (8, LANES), 1)
    for block in range(n_section // 4):
        label = jnp.broadcast_to(members[0:1, block * LANES : (block + 1) * LANES], (8, LANES))
        high, low = label // LANES, label % LANES
        found = jnp.zeros((8, LANES), jnp.float32)
        for col in range(columns):
            picked = jnp.take_along_axis(
                peaks[:, col * LANES : (col + 1) * LANES], low, axis=1, mode="promise_in_bounds"
            )
            found = jnp.where(high == col, picked, found)
        found = 1.0 / (found + EPSILON)
        turned = [found] + [pltpu.roll(found, 32 * q, 1) for q in range(1, 4)]
        for q in range(4):
            full = turned[(0 - q) % 4]
            for a in range(1, 4):
                full = jnp.where(lane // 32 == a, turned[(a - q) % 4], full)
            for f in range(FIELDS):
                scale[f, 4 * block + q] = full[f : f + 1]
    edges = fringe[...].reshape(4 * n_section, LANES)
    side = lax.broadcasted_iota(jnp.int32, edges.shape, 1)
    edges = jnp.where(side < 64, pltpu.roll(edges, 4 * n_section - 4, 0), pltpu.roll(edges, 4, 0))

    c = cosines()
    first = jnp.zeros(edges.shape, jnp.float32)
    final_cell = jnp.zeros(edges.shape, jnp.float32)
    for k in range(4):
        first = jnp.where(side == 32 * k, float(c[k, 0]), first)
        final_cell = jnp.where(side == 32 * k + 31, float(c[k, 3]), final_cell)
    for f in range(FIELDS):
        for k in range(PLANES):
            at = PLANES * f + k
            extra = final_cell * edges[:, at : at + 1] + first * edges[:, 64 + at : 65 + at]
            added[:, f, k] = extra.reshape(n_section, 4, LANES)

    def visit(b, carry):
        slot = slot_ref[0, b]
        columns_now = pl.ds(pl.multiple_of(slot * LANES, LANES), LANES)
        for f in range(FIELDS):
            coded[f, :, :, columns_now] = (landed[b, f] + added[b, f]) * scale[f, slot][None]
        return carry

    lax.fori_loop(0, n_section, visit, 0, unroll=4)


def per_device(density, momentum, energy, membership, slot_of_brick):
    planes, rows, width = density.shape
    n_section = rows // 4
    block_rows = -(-n_section // 8) * 8
    shards = CORES * Y_CHIPS
    depth = 64 // shards
    f32 = jnp.float32
    height = rows + 2 * EDGE
    vmem, anywhere = pl.BlockSpec(memory_space=pltpu.VMEM), pl.BlockSpec(memory_space=pl.ANY)
    smem = pl.BlockSpec(memory_space=pltpu.SMEM)
    dma = pltpu.SemaphoreType.DMA
    landed, fringe, final = pl.pallas_call(
        step_kernel,
        out_shape=(
            jax.ShapeDtypeStruct((n_section, FIELDS, planes, 4, width), f32),
            jax.ShapeDtypeStruct((n_section, 4, width), f32),
            jax.ShapeDtypeStruct((64, width), f32),
        ),
        in_specs=[vmem, anywhere, anywhere, anywhere, anywhere, vmem, vmem, vmem, vmem],
        out_specs=(anywhere, anywhere, vmem),
        scratch_shapes=[
            pltpu.VMEM((FIELDS, planes, height, width), f32),
            pltpu.VMEM((FIELDS, planes, height, width), f32),
            pltpu.VMEM((FIELDS, planes, height, width), f32),
            pltpu.VMEM((FIELDS, planes, height, width), f32),
            pltpu.VMEM((n_section, FIELDS, planes, 4, width), f32),
            pltpu.VMEM((2, FIELDS, planes, 4, width), f32),
            pltpu.VMEM((height, width), f32),
            pltpu.VMEM((FIELDS, planes, rows, width), f32),
            pltpu.VMEM((rows, width), f32),
            pltpu.VMEM((FIELDS * 32, width), f32),
            pltpu.VMEM((n_section, 4, width), f32),
            pltpu.VMEM((FIELDS, 4 * block_rows, width), f32),
            pltpu.VMEM((n_section, 1, membership.shape[1]), jnp.int32),
            pltpu.VMEM((n_section // 4, block_rows, width), jnp.int32),
            pltpu.VMEM((2, FIELDS, 8, width), f32),
            pltpu.VMEM((2, 3, FIELDS, 8, width), f32),
            pltpu.VMEM((2, 3, FIELDS, 8, width), f32),
            pltpu.VMEM((FIELDS, GROUPS // width, 8, width), f32),
            pltpu.VMEM((shards, depth, width), f32),
            pltpu.VMEM((shards - 1, depth, width), f32),
            pltpu.VMEM((max(X_CHIPS - 1, 1), depth, width), f32),
            pltpu.VMEM((Z_HI * Z_LO - 1, depth, width), f32),
            pltpu.VMEM((3, depth, width), f32),
            pltpu.VMEM((shards, depth, width), f32),
            dma((4,)),
            dma((2, 3)),
            dma((2, 3)),
            dma((2, 3)),
            dma((2, 3)),
            dma,
            dma,
            dma,
            dma,
            dma,
            dma,
            dma,
            dma,
            dma((4,)),
            dma((4,)),
        ],
        compiler_params=pltpu.CompilerParams(collective_id=0, has_side_effects=True),
        name="step",
    )(slot_of_brick, density, momentum, energy, membership, row_matrix(rows), brick_matrix(), depth_matrix(), outer_matrix(rows))
    return pl.pallas_call(
        place_kernel,
        out_shape=(
            jax.ShapeDtypeStruct((FIELDS, planes, 4, n_section * width), f32),
            jax.ShapeDtypeStruct((FIELDS, GROUPS), f32),
        ),
        in_specs=[smem, vmem, vmem, vmem, vmem],
        out_specs=(vmem, vmem),
        scratch_shapes=[
            pltpu.VMEM((8, GROUPS), f32),
            pltpu.VMEM((FIELDS, n_section, 1, width), f32),
            pltpu.VMEM((n_section, FIELDS, planes, 4, width), f32),
        ],
        name="place",
    )(slot_of_brick, final, membership, landed, fringe)


def solution(mesh):
    placed = (
        P(None, "sim", "section"),
        P(None, None, "sim", "section"),
        P(None, "sim", "section"),
        P(("sim", "section"), None),
        P("sim", None),
    )
    return jax.shard_map(
        per_device,
        mesh=mesh,
        in_specs=placed,
        out_specs=(P(None, None, ("sim", "section"), None), P()),
        check_vma=False,
    )
```
